32 devices in a mesh: slab: 8 (over z, y), grp: 4 (over x, core).
Axes of the slice: x: 2, y: 2, z: 4, core: 2. Of those that a mesh axis runs over, the one named last changes fastest.
Arguments:
- positions: float32 [32, 3, 8192], P(('slab', 'grp')), may hold values from 0 to 1
- masses: float32 [32, 8192], P(('slab', 'grp')), may hold values from 0.001 to 0.01
- smoothing: float32 [32, 8192], P(('slab', 'grp')), may hold values from 0.3 to 0.6
- block_lists: int32 [32, 64, 8], P(('slab', 'grp')), may hold values from 0 to 63, as said below
- block_counts: int32 [32, 8], P(('slab', 'grp')), may hold values from 0 to 128, as said below
- group_owner: int32 [4, 8], P('grp'), may hold values from 0 to 7, each once within a row
Outputs:
- density: float32 [32, 8192], P(('slab', 'grp'))
- potential: float32 [32, 8192], P(('slab', 'grp'))
- group_energy: float32 [4, 8], P('grp', 'slab')
The draws below stay inside these ranges and needn't reach their ends.
Inputs may be any that keep to these rules, and one draw needn't show every extreme that they name: `block_lists`: columns 0 to 1 name blocks of the slab below, the next 4 columns blocks of the own slab, the first of them the block itself, and the last 2 columns blocks of the slab above; the entries of each of these three sets differ. Block c of a slab lists block b of the slab below in its first 2 columns exactly when block b lists block c in its last 2 columns. `block_counts`: within one subgroup, a slab's rows begin with the members of its groups, group after group in order of group number. In every subgroup one group has 128 members on every slab.
All inputs are finite; a program needn't handle non-finite values.
Results may differ from the reference program's by a relative error of at most 0.0003.
Values sent between devices are 32-bit elements; how exact they have to be, the bound alone decides.
A program may use at most 64 MiB of HBM per device.

```python
import math
import jax
import jax.numpy as jnp
from jax import lax

TILE = 128
PB = 64
KX = 2
KO = 4
PARTS_DEV = 8192
NSP = 32
GROUPS = 8
N_SLAB = 8
N_GRP = 4


def draw_block_lists(key, part):
    cross_key = jax.random.fold_in(key, 11)
    own_key = jax.random.fold_in(key, 12)

    def permute_cross(sub_key):
        return jax.random.permutation(sub_key, PB)

    def permute_own(sub_key):
        return jax.random.permutation(sub_key, PB - 1)
    crossing = jax.vmap(permute_cross)(jax.random.split(cross_key, NSP)).astype(jnp.int32)
    inverse = jnp.argsort(crossing, axis=1).astype(jnp.int32)
    block_ids = jnp.arange(PB, dtype=jnp.int32)
    steps = jnp.arange(KX, dtype=jnp.int32)
    upward = crossing[:, (block_ids[:, None] + steps[None, :]) % PB]
    previous = jnp.roll(inverse, 1, axis=0)
    downward = (previous[:, :, None] - steps[None, None, :]) % PB
    offsets = jax.vmap(permute_own)(jax.random.split(own_key, NSP * PB)).astype(jnp.int32)
    offsets = offsets[:, :KO - 1].reshape(NSP, PB, KO - 1) + 1
    own_self = jnp.broadcast_to(block_ids[None, :, None], (NSP, PB, 1))
    own_other = (block_ids[None, :, None] + offsets) % PB
    return jnp.concatenate([downward, own_self, own_other, upward], axis=2).astype(jnp.int32)


def draw_block_counts(key, part):
    hottest = jax.random.randint(jax.random.fold_in(key, 21), (N_GRP,), 0, GROUPS)
    counts = jax.random.randint(jax.random.fold_in(key, 22), (NSP, GROUPS), 0, 2 * TILE // 3 + 1)
    subgroup = jnp.arange(NSP, dtype=jnp.int32) % N_GRP
    is_hot = jnp.arange(GROUPS, dtype=jnp.int32)[None, :] == hottest[subgroup][:, None]
    return jnp.where(is_hot, TILE, counts).astype(jnp.int32)


def level_of(key, shape, cuts, least, high):
    gain, own = 1.0, jax.random.fold_in(key, 6)
    for position, parts in cuts:
        heights = jnp.exp(jax.random.uniform(jax.random.fold_in(own, position), (parts,), jnp.float32, least / len(cuts), high / len(cuts)))
        gain = gain * jnp.repeat(heights, shape[position] // parts).reshape([-1 if axis == position else 1 for axis in range(len(shape))])
    return gain


def setup_inputs(seed: int = 0) -> dict:
    arg_keys = jax.random.split(jax.random.key(seed), 7)
    positions = jnp.clip(1.0 * jax.random.uniform(arg_keys[0], (NSP, 3, PARTS_DEV), jnp.float32) ** level_of(arg_keys[0], (NSP, 3, PARTS_DEV), ((0, 32),), -0.2, 0.2), 0.0, 1.0)
    masses = jnp.clip(jnp.exp(math.log(0.01) - 2.30258502 * jax.random.uniform(arg_keys[1], (NSP, PARTS_DEV), jnp.float32) ** level_of(arg_keys[1], (NSP, PARTS_DEV), ((0, 32),), -0.2, 0.2)), 0.001, 0.01)
    smoothing = jnp.clip(jnp.exp(math.log(0.6) - 0.6931472 * jax.random.uniform(arg_keys[2], (NSP, PARTS_DEV), jnp.float32) ** level_of(arg_keys[2], (NSP, PARTS_DEV), ((0, 32),), -0.2, 0.2)), 0.3, 0.6)
    block_lists = draw_block_lists(jax.random.fold_in(arg_keys[6], 71), 0)
    block_counts = draw_block_counts(jax.random.fold_in(arg_keys[6], 71), 0)
    group_owner = jax.vmap(lambda own: jax.random.permutation(own, N_SLAB))(jax.random.split(arg_keys[5], N_GRP)).reshape((N_GRP, GROUPS)).astype(jnp.int32)
    return {"positions": positions, "masses": masses, "smoothing": smoothing, "block_lists": block_lists, "block_counts": block_counts, "group_owner": group_owner}


KERNEL_NORM = 21.0 / (16.0 * math.pi)

def kernel_tile(target, source):
    delta_x = target[..., 0, :, None] - source[..., 0, None, :]
    delta_y = target[..., 1, :, None] - source[..., 1, None, :]
    delta_z = target[..., 2, :, None] - source[..., 2, None, :]
    pair_size = 0.5 * (target[..., 4, :, None] + source[..., 4, None, :])
    scaled = jnp.sqrt(delta_x * delta_x + delta_y * delta_y + delta_z * delta_z) / pair_size
    falloff = jnp.maximum(1.0 - 0.5 * scaled, 0.0)
    falloff_sq = falloff * falloff
    return KERNEL_NORM / (pair_size * pair_size * pair_size) * falloff_sq * falloff_sq * (1.0 + 2.0 * scaled)

def to_blocks(particles):
    return particles.reshape(5, PB, TILE).transpose(1, 0, 2)

def group_potential(members):
    total_rows = members.shape[1]
    width = min(512, total_rows)
    softness = 0.25 * members[4] * members[4]

    def row_block(start):
        target = lax.dynamic_slice_in_dim(members, start, width, 1)
        target_soft = lax.dynamic_slice_in_dim(softness, start, width, 0)
        delta_x = target[0][:, None] - members[0][None, :]
        delta_y = target[1][:, None] - members[1][None, :]
        delta_z = target[2][:, None] - members[2][None, :]
        inverse = lax.rsqrt(delta_x * delta_x + delta_y * delta_y + delta_z * delta_z + 0.5 * (target_soft[:, None] + softness[None, :]))
        summed = lax.optimization_barrier(jnp.sum(inverse * members[3][None, :], axis=1))
        return target[3] * lax.rsqrt(target_soft) - summed
    starts = jnp.arange(total_rows // width, dtype=jnp.int32) * width
    return lax.map(row_block, starts).reshape(total_rows)

def reference(positions, masses, smoothing, block_lists, block_counts, group_owner):
    particles = jnp.concatenate([positions, masses[:, None, :], smoothing[:, None, :]], axis=1)
    slabs = particles.shape[0]
    row_count = particles.shape[2]
    blocks = jax.vmap(to_blocks)(particles)
    offset_x = jnp.array([1.0, 0.0, 0.0, 0.0, 0.0], jnp.float32)[:, None]
    lower = jnp.roll(blocks, 1, axis=0) - offset_x
    upper = jnp.roll(blocks, -1, axis=0) + offset_x
    candidates = jnp.concatenate([lower, blocks, upper], axis=1)
    column_base = jnp.concatenate([jnp.zeros((KX,), jnp.int32), jnp.full((KO,), PB, jnp.int32), jnp.full((KX,), 2 * PB, jnp.int32)])

    def one_slab(pieces):
        slab_cands, own_blocks, slab_lists = pieces
        picked = slab_cands[(slab_lists + column_base[None, :]).astype(jnp.int32)]

        def one_block(couple):
            target, sources = couple
            flat_src = sources.transpose(1, 0, 2).reshape(5, -1)
            return lax.optimization_barrier(jnp.sum(kernel_tile(target, flat_src) * flat_src[3][None, :], axis=1))
        return lax.map(one_block, (own_blocks, picked))
    density = lax.map(one_slab, (candidates, blocks, block_lists)).reshape(slabs, row_count)
    offsets = (jnp.cumsum(block_counts, axis=1) - block_counts).astype(jnp.int32)
    slot = jnp.arange(TILE, dtype=jnp.int32)
    row_index = jnp.minimum(offsets[:, :, None] + slot[None, None, :], row_count - 1).astype(jnp.int32)
    live = slot[None, None, :] < block_counts[:, :, None]

    def pick_rows(slab_parts, slab_index):
        return jnp.take(slab_parts, slab_index.reshape(-1), axis=1)
    picked = jax.vmap(pick_rows)(particles, row_index).reshape(slabs, 5, GROUPS, TILE)
    masked = jnp.where(live, picked[:, 3], 0.0)
    picked = jnp.concatenate([picked[:, :3], masked[:, None], picked[:, 4:]], axis=1)
    by_group = picked.reshape(N_SLAB, N_GRP, 5, GROUPS, TILE).transpose(1, 3, 2, 0, 4)
    members = by_group.reshape(N_GRP * GROUPS, 5, N_SLAB * TILE)

    def one_group(group_rows):
        values = group_potential(group_rows)
        return (values, 0.5 * jnp.sum(group_rows[3] * values))
    potentials, energies = lax.map(one_group, members)
    returned = potentials.reshape(N_GRP, GROUPS, N_SLAB, TILE).transpose(2, 0, 1, 3)
    returned = returned.reshape(slabs, GROUPS * TILE)
    ends = (offsets + block_counts).astype(jnp.int32)
    all_rows = jnp.arange(row_count, dtype=jnp.int32)

    def one_map(pieces):
        slab_ends, slab_offsets, table = pieces
        member_of = lax.optimization_barrier(jnp.sum((slab_ends[None, :] <= all_rows[:, None]).astype(jnp.int32), axis=1)).astype(jnp.int32)
        bounded = jnp.minimum(member_of, GROUPS - 1)
        first_row = slab_offsets[bounded]
        flat_index = (bounded * TILE + jnp.clip(all_rows - first_row, 0, TILE - 1)).astype(jnp.int32)
        return jnp.where(member_of < GROUPS, table[flat_index], 0.0)
    potential = lax.map(one_map, (ends, offsets, returned))
    subgroup = jnp.arange(N_GRP, dtype=jnp.int32)[:, None]
    group_energy = jnp.zeros((N_GRP, N_SLAB), jnp.float32).at[subgroup, group_owner].set(energies.reshape(N_GRP, GROUPS))
    return (density, potential, group_energy)
```

```python
import functools
import math

import jax
import jax.numpy as jnp
from jax import lax
from jax.experimental import pallas as pl
from jax.experimental.pallas import tpu as pltpu
from jax.sharding import PartitionSpec as P

TILE = 128
KX = 2
KO = 4
F32 = jnp.float32
HALF = jnp.bfloat16
DEPTH = 64
LOT = 8

DENSITY_SCALE = 21.0 / (256.0 * math.pi) / 16.0

VMEM = pl.BlockSpec(memory_space=pltpu.VMEM)
MESH = pl.DeviceIdType.MESH
SMEM = pl.BlockSpec(memory_space=pltpu.SMEM)


def split3(a):
    high = a.astype(HALF).astype(F32)
    rest = a - high
    mid = rest.astype(HALF).astype(F32)
    return high, mid, rest - mid


def left_six(a):
    high, mid, low = split3(a)
    return [high, high, mid, high, low, mid]


def right_six(a):
    high, mid, low = split3(a)
    return [high, mid, high, low, high, mid]


def left_rows(a):
    return jnp.concatenate(left_six(a), axis=0).astype(HALF)


def right_rows(a):
    return jnp.concatenate(right_six(a), axis=0).astype(HALF)


def centred(particles, lift):
    row = lax.broadcasted_iota(jnp.int32, particles.shape, 0)
    shift = jnp.where(row == 0, lift - 0.5, jnp.where(row < 3, -0.5, 0.0))
    coords = jnp.where(row < 3, particles + shift, 0.0)
    norm = jnp.sum(coords * coords, axis=0, keepdims=True)
    return row, coords, norm


FACTORS = 8
NORM, SIZE, PLANES = 8, 11, 14


def fill_planes(parts, plane_ref, lift):
    place_ref, mass_ref, size_ref = parts

    def step(i, _):
        rows = pl.ds(pl.multiple_of(i * LOT, LOT), LOT)
        coords = [place_ref[axis, rows, :] + ((lift if axis == 0 else 0.0) - 0.5) for axis in range(3)]
        norm = coords[0] * coords[0] + coords[1] * coords[1] + coords[2] * coords[2]
        size = size_ref[rows, :]
        planes = coords + [lax.rsqrt(mass_ref[rows, :])]
        for _ in range(4):
            planes.append(planes[-1] * size)
        planes += list(split3(norm)) + list(split3(size))
        for n, plane in enumerate(planes):
            plane_ref[n, rows, :] = plane
        return 0

    lax.fori_loop(0, mass_ref.shape[0] // LOT, step, 0, unroll=2)


def by_row(values):
    row = lax.broadcasted_iota(jnp.int32, (8, TILE), 0)
    block = jnp.broadcast_to(values[0], (8, TILE))
    for n, value in enumerate(values[1:]):
        block = jnp.where(row == n + 1, value, block)
    return block


def fill(parts, plane_ref, left_ref, right_ref, lift):
    fill_planes(parts, plane_ref, lift)
    row = lax.broadcasted_iota(jnp.int32, (8, TILE), 0)
    zero = jnp.zeros((8, TILE), F32)

    def step(i, _):
        plane = [plane_ref[n, pl.ds(i, 1), :] for n in range(PLANES)]
        coords, powers, norm, size = plane[:3], plane[3:8], plane[NORM:SIZE], plane[SIZE:]
        if left_ref is not None:
            high, mid, low = split3(by_row(coords + powers[::-1]))
            rest = by_row(norm + [1.0, 1.0, 1.0] + size[:2])
            last = jnp.where(row == 0, size[2], 0.0)
            left_ref[i] = jnp.concatenate([high, high, high, mid, mid, low, rest, last], axis=0).T.astype(HALF)
        scale = by_row([-8.0, -8.0, -8.0, 0.0625, 0.25, 0.375, 0.25, 0.0625])
        parts3 = split3(scale * by_row(coords + powers))
        near = [jnp.where(row < 3, part, 0.0) for part in parts3]
        far = [jnp.where(row < 3, 0.0, part) for part in parts3]
        order = (0, 1, 2, 0, 1, 0)
        rest = by_row([4.0, 4.0, 4.0] + [4.0 * part for part in norm] + [0.0, 0.0])
        wide = by_row([0.0, 0.0, 0.0] + [2.0 * part for part in size] + [2.0, 2.0])
        last = jnp.where(row == 0, 2.0, 0.0)
        columns = (
            [near[n] for n in order] + [rest, zero],
            [zero] * 6 + [wide, last],
            [far[n] for n in order] + [zero, zero],
        )
        for m, column in enumerate(columns):
            right_ref[i, :, pl.ds(m * TILE, TILE)] = jnp.concatenate(column, axis=0).astype(HALF)
        return 0

    lax.fori_loop(0, right_ref.shape[0], step, 0, unroll=4)


def pair_dot(left, right, left_dim=0):
    return lax.dot_general(
        left, right, (((left_dim,), (0,)), ((), ())), preferred_element_type=F32
    )


def weights(both_ref, k):
    rows = pl.ds(k * TILE, TILE)
    squared = jnp.maximum(both_ref[rows, :TILE], 1e-30)
    reach = both_ref[rows, TILE : 2 * TILE]
    near = jnp.maximum(reach - squared * lax.rsqrt(squared), 0.0)
    a = near * lax.rsqrt(both_ref[rows, 2 * TILE : 3 * TILE])
    a = a * a
    return (a * a) * (1.25 * reach - near)


def sweep(first, last, fetch, use, even_ref, odd_ref, unroll=4):
    fetch(first, even_ref)

    def step(i, _):
        b = first + 2 * i
        fetch(b + 1, odd_ref)
        use(b, even_ref)
        fetch(jnp.minimum(b + 2, last - 1), even_ref)
        use(b + 1, odd_ref)
        return 0

    lax.fori_loop(0, (last - first) // 2, step, 0, unroll=unroll)


def own_part(first, last, list_ref, dens_ref, left_ref, right_ref, even_ref, odd_ref):
    def fetch(b, both_ref):
        right = right_ref[b]
        for k in range(KO):
            both_ref[pl.ds(k * TILE, TILE), :] = pair_dot(left_ref[list_ref[KX + k, b]], right, 1)

    def use(b, both_ref):
        total = jnp.zeros((8, TILE), F32)
        for k in range(KO):
            total = total + jnp.sum(weights(both_ref, k).reshape(TILE // 8, 8, TILE), axis=0)
        dens_ref[pl.ds(b, 1), :] += jnp.sum(total, axis=0, keepdims=True)

    sweep(first, last, fetch, use, even_ref, odd_ref)


def cross_part(list_ref, dens_ref, column_ref, back_ref, left_ref, right_ref, even_ref, odd_ref):
    blocks = left_ref.shape[0]

    def fetch(b, both_ref):
        left = left_ref[b]
        for k in range(KX):
            both_ref[pl.ds(k * TILE, TILE), :] = pair_dot(left, right_ref[list_ref[KX + KO + k, b]], 1)

    def use(b, both_ref):
        total = None
        for k in range(KX):
            value = weights(both_ref, k)
            total = value if total is None else total + value
            column_ref[pl.ds(KX * b + k, 1), :] = jnp.sum(value, axis=0, keepdims=True)
        dens_ref[pl.ds(b, 1), :] += jnp.sum(total.T, axis=0, keepdims=True)

    sweep(0, blocks, fetch, use, even_ref, odd_ref)

    lane = lax.broadcasted_iota(jnp.int32, (1, KX * blocks), 1)

    def name(b, row):
        for k in range(KX):
            row = jnp.where(lane == KX * b + k, list_ref[KX + KO + k, b], row)
        return row

    named = lax.fori_loop(0, blocks, name, jnp.zeros((1, KX * blocks), jnp.int32), unroll=8)
    block = lax.broadcasted_iota(jnp.int32, (blocks, KX * blocks), 0)
    chosen = jnp.where(block == named, 1.0, 0.0).astype(HALF)
    high, mid, low = split3(column_ref[...])
    back_ref[...] = sum(
        jnp.dot(chosen, part.astype(HALF), preferred_element_type=F32) for part in (low, mid, high)
    )


def main_kernel(
    slabs,
    grps,
    place_ref,
    weight_ref,
    size_ref,
    group_ref,
    list_ref,
    dens_ref,
    table_ref,
    back_ref,
    energy_ref,
    far_place_ref,
    far_weight_ref,
    far_size_ref,
    member_ref,
    phi_ref,
    column_ref,
    sent_ref,
    left_ref,
    right_ref,
    far_ref,
    even_ref,
    odd_ref,
    near_even_ref,
    near_odd_ref,
    phi_target_ref,
    phi_source_ref,
    plane_ref,
    member_send,
    member_recv,
    phi_send,
    phi_recv,
    part_send,
    part_recv,
    back_send,
    back_recv,
):
    slab = lax.axis_index("slab")
    grp = lax.axis_index("grp")
    count = slabs * grps
    here = slab * grps + grp

    def place(index):
        return (index // grps, lax.rem(index, grps))

    above = place(lax.rem(here + 1, count))
    below = place(lax.rem(here + count - 1, count))

    def ahead(d):
        return lax.rem(slab + d, slabs)

    barrier = pltpu.get_barrier_semaphore()
    for other in (above, below):
        pl.semaphore_signal(barrier, inc=1, device_id=other, device_id_type=MESH)

    def greet(d, _):
        pl.semaphore_signal(barrier, inc=1, device_id=(ahead(d), grp), device_id_type=MESH)
        return 0

    lax.fori_loop(1, slabs, greet, 0)
    parts = (place_ref, weight_ref, size_ref)
    far_parts = (far_place_ref, far_weight_ref, far_size_ref)
    blocks = dens_ref.shape[0]
    early = blocks // 8 * 2
    later = blocks // 4 * 2
    own = (list_ref, dens_ref, left_ref, right_ref, even_ref, odd_ref)
    dens_ref[...] = jnp.zeros_like(dens_ref)
    fill(parts, plane_ref, left_ref, right_ref, 0.0)
    own_part(0, early, *own)
    pl.semaphore_wait(barrier, slabs + 1)

    def member_copy(d):
        return pltpu.make_async_remote_copy(
            src_ref=group_ref.at[ahead(d)],
            dst_ref=member_ref.at[slab],
            send_sem=member_send.at[d],
            recv_sem=member_recv.at[d],
            device_id=(ahead(d), grp),
            device_id_type=MESH,
        )

    def phi_copy(d):
        return pltpu.make_async_remote_copy(
            src_ref=phi_ref.at[ahead(d)],
            dst_ref=table_ref.at[slab],
            send_sem=phi_send.at[d],
            recv_sem=phi_recv.at[d],
            device_id=(ahead(d), grp),
            device_id_type=MESH,
        )

    part_copies = [
        pltpu.make_async_remote_copy(
            src_ref=near,
            dst_ref=far,
            send_sem=part_send.at[n],
            recv_sem=part_recv.at[n],
            device_id=below,
            device_id_type=MESH,
        )
        for n, (near, far) in enumerate(zip(parts, far_parts))
    ]
    back_copy = pltpu.make_async_remote_copy(
        src_ref=sent_ref,
        dst_ref=back_ref,
        send_sem=back_send,
        recv_sem=back_recv,
        device_id=above,
        device_id_type=MESH,
    )

    def each(action):
        def step(d, _):
            action(d)
            return 0

        lax.fori_loop(1, slabs, step, 0)

    each(lambda d: member_copy(d).start())
    for copy in part_copies:
        copy.start()

    own_part(early, later, *own)

    for copy in part_copies:
        copy.wait()
    fill(far_parts, plane_ref, None, far_ref, 1.0)
    cross_part(list_ref, dens_ref, column_ref, sent_ref, left_ref, far_ref, near_even_ref, near_odd_ref)
    back_copy.start()

    member_ref[slab] = group_ref[slab]
    each(lambda d: member_copy(d).wait())
    phi_part(member_ref, phi_ref, energy_ref, phi_target_ref, phi_source_ref)
    each(lambda d: phi_copy(d).start())
    table_ref[slab] = phi_ref[slab]

    own_part(later, blocks, *own)
    each(lambda d: phi_copy(d).wait())
    back_copy.wait()


def block_of(parts, i):
    place_ref, mass_ref, size_ref = parts
    row = lax.broadcasted_iota(jnp.int32, (8, TILE), 0)
    block = jnp.broadcast_to(size_ref[pl.ds(i, 1), :], (8, TILE))
    block = jnp.where(row == 3, mass_ref[pl.ds(i, 1), :], block)
    for axis in range(3):
        block = jnp.where(row == axis, place_ref[axis, pl.ds(i, 1), :], block)
    return block


def pick_kernel(place_ref, weight_ref, size_ref, count_ref, owner_ref, out_ref):
    parts = (place_ref, weight_ref, size_ref)
    blocks = weight_ref.shape[0]
    row = lax.broadcasted_iota(jnp.int32, (8, TILE), 0)
    lane = lax.broadcasted_iota(jnp.int32, (8, TILE), 1)

    def step(k, start):
        count = count_ref[0, k]
        block = jnp.minimum(start // TILE, blocks - 1)
        shift = start % TILE
        after = jnp.minimum(block + 1, blocks - 1)
        first = block_of(parts, block)
        second = block_of(parts, after)
        mixed = pltpu.roll(jnp.where(lane >= shift, first, second), (TILE - shift) % TILE, 1)
        out_ref[owner_ref[0, k]] = jnp.where((row == 3) & (lane >= count), 0.0, mixed)
        return start + count

    lax.fori_loop(0, count_ref.shape[1], step, jnp.int32(0), unroll=8)


def phi_part(member_ref, phi_ref, energy_ref, target_ref, source_ref):
    slabs = member_ref.shape[0]
    group = math.gcd(slabs, 8)

    def fill(i, _):
        particles = member_ref[i]
        row, coords, norm = centred(particles, 0.0)
        size = particles[4:5]
        norm = norm + 0.125 * size * size
        base = pl.multiple_of(i * TILE, TILE)
        source_ref[:, pl.ds(base, TILE)] = right_rows(
            jnp.where(row < 3, coords, jnp.where(row == 3, norm, jnp.where(row == 4, 1.0, 0.0)))
        )
        target_ref[:, pl.ds(base, TILE)] = left_rows(
            jnp.where(row < 3, -2.0 * coords, jnp.where(row == 3, 1.0, jnp.where(row == 4, norm, 0.0)))
        )
        return 0

    lax.fori_loop(0, slabs, fill, 0)

    def step(i, energy):
        target = target_ref[:, pl.ds(pl.multiple_of(i * TILE, TILE), TILE)]

        def inner(j, total):
            for n in range(group):
                base = pl.multiple_of((j * group + n) * TILE, TILE)
                pairs = pair_dot(target, source_ref[:, pl.ds(base, TILE)])
                total = total + lax.rsqrt(pairs) * member_ref[j * group + n, 3:4, :]
            return total

        total = lax.fori_loop(0, slabs // group, inner, jnp.zeros((TILE, TILE), F32), unroll=slabs == group)
        mass = member_ref[i, 3:4, :]
        size = member_ref[i, 4:5, :]
        phi = mass * (2.0 / size) - jnp.sum(total.T, axis=0, keepdims=True)
        phi_ref[i] = phi
        return energy + mass * phi

    energy = lax.fori_loop(0, slabs, step, jnp.zeros((1, TILE), F32), unroll=4 if slabs == group else 1)
    energy_ref[...] = 0.5 * jnp.sum(energy, axis=1, keepdims=True)


def final_kernel(mass_ref, dens_ref, back_ref, table_ref, count_ref, owner_ref, out_ref, pot_ref, work_ref):
    out_ref[...] = (dens_ref[...] + back_ref[...]) * (DENSITY_SCALE / mass_ref[...])
    work_ref[...] = jnp.zeros_like(work_ref)
    lane = lax.broadcasted_iota(jnp.int32, (1, TILE), 1)

    def step(k, start):
        count = count_ref[0, k]
        block = start // TILE
        shift = start % TILE
        value = table_ref[owner_ref[0, k]]
        value = pltpu.roll(jnp.where(lane < count, value, 0.0), shift, 1)
        work_ref[pl.ds(block, 1), :] += jnp.where(lane >= shift, value, 0.0)
        work_ref[pl.ds(block + 1, 1), :] += jnp.where(lane < shift, value, 0.0)
        return start + count

    lax.fori_loop(0, count_ref.shape[1], step, jnp.int32(0), unroll=8)
    pot_ref[...] = work_ref[: pot_ref.shape[0], :]


def per_device(positions, masses, smoothing, block_lists, block_counts, group_owner):
    row_count = masses.shape[1]
    blocks = row_count // TILE
    groups = block_counts.shape[1]
    slabs = lax.axis_size("slab")
    grps = lax.axis_size("grp")
    particles = (
        positions[0].reshape(3, blocks, TILE),
        masses.reshape(blocks, TILE),
        smoothing.reshape(blocks, TILE),
    )
    outgoing = pl.pallas_call(
        pick_kernel,
        out_shape=jax.ShapeDtypeStruct((groups, 8, TILE), F32),
        in_specs=[VMEM, VMEM, VMEM, SMEM, SMEM],
        out_specs=VMEM,
    )(*particles, block_counts, group_owner)

    grid_shape = jax.ShapeDtypeStruct((blocks, TILE), F32)
    row_shape = jax.ShapeDtypeStruct((slabs, 1, TILE), F32)
    dma = pltpu.SemaphoreType.DMA
    density, table, back, energy = pl.pallas_call(
        functools.partial(main_kernel, slabs, grps),
        out_shape=(grid_shape, row_shape, grid_shape, jax.ShapeDtypeStruct((1, 1), F32)),
        in_specs=[VMEM, VMEM, VMEM, VMEM, SMEM],
        out_specs=(VMEM, VMEM, VMEM, VMEM),
        scratch_shapes=[
            pltpu.VMEM((3, blocks, TILE), F32),
            pltpu.VMEM((blocks, TILE), F32),
            pltpu.VMEM((blocks, TILE), F32),
            pltpu.VMEM((slabs, 8, TILE), F32),
            pltpu.VMEM((slabs, 1, TILE), F32),
            pltpu.VMEM((KX * blocks, TILE), F32),
            pltpu.VMEM((blocks, TILE), F32),
            pltpu.VMEM((blocks, TILE, DEPTH), HALF),
            pltpu.VMEM((blocks, DEPTH, 3 * TILE), HALF),
            pltpu.VMEM((blocks, DEPTH, 3 * TILE), HALF),
            pltpu.VMEM((KO * TILE, 3 * TILE), F32),
            pltpu.VMEM((KO * TILE, 3 * TILE), F32),
            pltpu.VMEM((KX * TILE, 3 * TILE), F32),
            pltpu.VMEM((KX * TILE, 3 * TILE), F32),
            pltpu.VMEM((48, slabs * TILE), HALF),
            pltpu.VMEM((48, slabs * TILE), HALF),
            pltpu.VMEM((PLANES, blocks, TILE), F32),
            dma((slabs,)),
            dma((slabs,)),
            dma((slabs,)),
            dma((slabs,)),
            dma((3,)),
            dma((3,)),
            dma,
            dma,
        ],
        compiler_params=pltpu.CompilerParams(collective_id=0, has_side_effects=True),
    )(*particles, outgoing, block_lists[0].T)
    density, potential = pl.pallas_call(
        final_kernel,
        out_shape=(grid_shape, grid_shape),
        in_specs=[VMEM, VMEM, VMEM, VMEM, SMEM, SMEM],
        out_specs=(VMEM, VMEM),
        scratch_shapes=[pltpu.VMEM((blocks + 8, TILE), F32)],
    )(particles[1], density, back, table, block_counts, group_owner)
    return (density.reshape(1, row_count), potential.reshape(1, row_count), energy)


def solution(mesh):
    placed = (
        P(("slab", "grp"), None, None),
        P(("slab", "grp"), None),
        P(("slab", "grp"), None),
        P(("slab", "grp"), None, None),
        P(("slab", "grp"), None),
        P("grp", None),
    )
    return jax.shard_map(
        per_device,
        mesh=mesh,
        in_specs=placed,
        out_specs=(P(("slab", "grp"), None), P(("slab", "grp"), None), P("grp", "slab")),
        check_vma=False,
    )
```

```python
import functools
import math

import jax
import jax.numpy as jnp
from jax import lax
from jax.experimental import pallas as pl
from jax.experimental.pallas import tpu as pltpu
from jax.sharding import PartitionSpec as P

TILE = 128
KX = 2
KO = 4
F32 = jnp.float32
HALF = jnp.bfloat16
DEPTH = 64
LOT = 8

DENSITY_SCALE = 21.0 / (256.0 * math.pi) / 16.0

VMEM = pl.BlockSpec(memory_space=pltpu.VMEM)
MESH = pl.DeviceIdType.MESH
SMEM = pl.BlockSpec(memory_space=pltpu.SMEM)


def split3(a):
    high = a.astype(HALF).astype(F32)
    rest = a - high
    mid = rest.astype(HALF).astype(F32)
    return high, mid, rest - mid


def left_six(a):
    high, mid, low = split3(a)
    return [high, high, mid, high, low, mid]


def right_six(a):
    high, mid, low = split3(a)
    return [high, mid, high, low, high, mid]


def left_rows(a):
    return jnp.concatenate(left_six(a), axis=0).astype(HALF)


def right_rows(a):
    return jnp.concatenate(right_six(a), axis=0).astype(HALF)


def centred(particles, lift):
    row = lax.broadcasted_iota(jnp.int32, particles.shape, 0)
    shift = jnp.where(row == 0, lift - 0.5, jnp.where(row < 3, -0.5, 0.0))
    coords = jnp.where(row < 3, particles + shift, 0.0)
    norm = jnp.sum(coords * coords, axis=0, keepdims=True)
    return row, coords, norm


FACTORS = 8
NORM, SIZE, PLANES = 8, 11, 14


def fill_planes(parts, plane_ref, lift):
    place_ref, mass_ref, size_ref = parts

    def step(i, _):
        rows = pl.ds(pl.multiple_of(i * LOT, LOT), LOT)
        coords = [place_ref[axis, rows, :] + ((lift if axis == 0 else 0.0) - 0.5) for axis in range(3)]
        norm = coords[0] * coords[0] + coords[1] * coords[1] + coords[2] * coords[2]
        size = size_ref[rows, :]
        planes = coords + [lax.rsqrt(mass_ref[rows, :])]
        for _ in range(4):
            planes.append(planes[-1] * size)
        planes += list(split3(norm)) + list(split3(size))
        for n, plane in enumerate(planes):
            plane_ref[n, rows, :] = plane
        return 0

    lax.fori_loop(0, mass_ref.shape[0] // LOT, step, 0, unroll=2)


def by_row(values):
    row = lax.broadcasted_iota(jnp.int32, (8, TILE), 0)
    block = jnp.broadcast_to(values[0], (8, TILE))
    for n, value in enumerate(values[1:]):
        block = jnp.where(row == n + 1, value, block)
    return block


def fill(parts, plane_ref, left_ref, right_ref, lift):
    fill_planes(parts, plane_ref, lift)
    row = lax.broadcasted_iota(jnp.int32, (8, TILE), 0)
    zero = jnp.zeros((8, TILE), F32)

    def step(i, _):
        plane = [plane_ref[n, pl.ds(i, 1), :] for n in range(PLANES)]
        coords, powers, norm, size = plane[:3], plane[3:8], plane[NORM:SIZE], plane[SIZE:]
        if left_ref is not None:
            high, mid, low = split3(by_row(coords + powers[::-1]))
            rest = by_row(norm + [1.0, 1.0, 1.0] + size[:2])
            last = jnp.where(row == 0, size[2], 0.0)
            left_ref[i] = jnp.concatenate([high, high, high, mid, mid, low, rest, last], axis=0).T.astype(HALF)
        scale = by_row([-8.0, -8.0, -8.0, 0.0625, 0.25, 0.375, 0.25, 0.0625])
        parts3 = split3(scale * by_row(coords + powers))
        near = [jnp.where(row < 3, part, 0.0) for part in parts3]
        far = [jnp.where(row < 3, 0.0, part) for part in parts3]
        order = (0, 1, 2, 0, 1, 0)
        rest = by_row([4.0, 4.0, 4.0] + [4.0 * part for part in norm] + [0.0, 0.0])
        wide = by_row([0.0, 0.0, 0.0] + [2.0 * part for part in size] + [2.0, 2.0])
        last = jnp.where(row == 0, 2.0, 0.0)
        columns = (
            [near[n] for n in order] + [rest, zero],
            [zero] * 6 + [wide, last],
            [far[n] for n in order] + [zero, zero],
        )
        for m, column in enumerate(columns):
            right_ref[i, :, pl.ds(m * TILE, TILE)] = jnp.concatenate(column, axis=0).astype(HALF)
        return 0

    lax.fori_loop(0, right_ref.shape[0], step, 0, unroll=4)


def pair_dot(left, right, left_dim=0):
    return lax.dot_general(
        left, right, (((left_dim,), (0,)), ((), ())), preferred_element_type=F32
    )


def weights(both_ref, base):
    rows = pl.ds(base, 8)
    squared = jnp.maximum(both_ref[rows, :TILE], 1e-30)
    reach = both_ref[rows, TILE : 2 * TILE]
    near = jnp.maximum(reach - squared * lax.rsqrt(squared), 0.0)
    a = near * lax.rsqrt(both_ref[rows, 2 * TILE : 3 * TILE])
    a = a * a
    return (a * a) * (1.25 * reach - near)


def sweep(first, last, end, fetch, use, even_ref, odd_ref, unroll):
    def step(i, _):
        b = first + 2 * i
        fetch(b + 1, odd_ref)
        use(b, even_ref)
        fetch(jnp.minimum(b + 2, end - 1), even_ref)
        use(b + 1, odd_ref)
        return 0

    lax.fori_loop(0, (last - first) // 2, step, 0, unroll=unroll)


def steps_of(first, last, most):
    return math.gcd((last - first) // 2, most)


def own_part(first, last, list_ref, dens_ref, left_ref, right_ref, even_ref, odd_ref):
    def fetch(b, both_ref):
        right = right_ref[b]
        for k in range(KO):
            both_ref[pl.ds(k * TILE, TILE), :] = pair_dot(left_ref[list_ref[KX + k, b]], right, 1)

    def use(b, both_ref):
        total = jnp.zeros((8, TILE), F32)
        for base in range(0, KO * TILE, 8):
            total = total + weights(both_ref, base)
        dens_ref[pl.ds(b, 1), :] += jnp.sum(total, axis=0, keepdims=True)

    if first == 0:
        fetch(0, even_ref)
    sweep(first, last, left_ref.shape[0], fetch, use, even_ref, odd_ref, steps_of(first, last, 12 if (last - first) % 3 == 0 else 8))


def cross_part(list_ref, dens_ref, column_ref, back_ref, left_ref, right_ref, even_ref, odd_ref):
    blocks = left_ref.shape[0]

    def fetch(b, both_ref):
        left = left_ref[b]
        for k in range(KX):
            both_ref[pl.ds(k * TILE, TILE), :] = pair_dot(left, right_ref[list_ref[KX + KO + k, b]], 1)

    def use(b, both_ref):
        column = [jnp.zeros((8, TILE), F32)] * KX
        total = []
        for base in range(0, TILE, 8):
            values = [weights(both_ref, k * TILE + base) for k in range(KX)]
            column = [old + value for old, value in zip(column, values)]
            total.append(sum(values))
        for k in range(KX):
            column_ref[pl.ds(KX * b + k, 1), :] = jnp.sum(column[k], axis=0, keepdims=True)
        total = jnp.concatenate(total, axis=0)
        dens_ref[pl.ds(b, 1), :] += jnp.sum(total.T, axis=0, keepdims=True)

    fetch(0, even_ref)
    sweep(0, blocks, blocks, fetch, use, even_ref, odd_ref, steps_of(0, blocks, 8))

    lane = lax.broadcasted_iota(jnp.int32, (1, KX * blocks), 1)

    def name(b, row):
        for k in range(KX):
            row = jnp.where(lane == KX * b + k, list_ref[KX + KO + k, b], row)
        return row

    named = lax.fori_loop(0, blocks, name, jnp.zeros((1, KX * blocks), jnp.int32), unroll=8)
    block = lax.broadcasted_iota(jnp.int32, (blocks, KX * blocks), 0)
    chosen = jnp.where(block == named, 1.0, 0.0).astype(HALF)
    high, mid, low = split3(column_ref[...])
    back_ref[...] = sum(
        jnp.dot(chosen, part.astype(HALF), preferred_element_type=F32) for part in (low, mid, high)
    )


def main_kernel(
    slabs,
    grps,
    place_ref,
    weight_ref,
    size_ref,
    group_ref,
    list_ref,
    dens_ref,
    table_ref,
    back_ref,
    energy_ref,
    far_place_ref,
    far_weight_ref,
    far_size_ref,
    member_ref,
    phi_ref,
    column_ref,
    sent_ref,
    left_ref,
    right_ref,
    far_ref,
    even_ref,
    odd_ref,
    near_even_ref,
    near_odd_ref,
    phi_target_ref,
    phi_source_ref,
    plane_ref,
    member_send,
    member_recv,
    phi_send,
    phi_recv,
    part_send,
    part_recv,
    back_send,
    back_recv,
):
    slab = lax.axis_index("slab")
    grp = lax.axis_index("grp")
    count = slabs * grps
    here = slab * grps + grp

    def place(index):
        return (index // grps, lax.rem(index, grps))

    above = place(lax.rem(here + 1, count))
    below = place(lax.rem(here + count - 1, count))

    def ahead(d):
        return lax.rem(slab + d, slabs)

    barrier = pltpu.get_barrier_semaphore()
    for other in (above, below):
        pl.semaphore_signal(barrier, inc=1, device_id=other, device_id_type=MESH)

    def greet(d, _):
        pl.semaphore_signal(barrier, inc=1, device_id=(ahead(d), grp), device_id_type=MESH)
        return 0

    lax.fori_loop(1, slabs, greet, 0)
    parts = (place_ref, weight_ref, size_ref)
    far_parts = (far_place_ref, far_weight_ref, far_size_ref)
    blocks = dens_ref.shape[0]
    early = blocks // 16 * 2
    later = blocks // 4 * 2
    own = (list_ref, dens_ref, left_ref, right_ref, even_ref, odd_ref)
    dens_ref[...] = jnp.zeros_like(dens_ref)
    fill(parts, plane_ref, left_ref, right_ref, 0.0)
    own_part(0, early, *own)
    pl.semaphore_wait(barrier, slabs + 1)

    def member_copy(d):
        return pltpu.make_async_remote_copy(
            src_ref=group_ref.at[ahead(d)],
            dst_ref=member_ref.at[slab],
            send_sem=member_send.at[d],
            recv_sem=member_recv.at[d],
            device_id=(ahead(d), grp),
            device_id_type=MESH,
        )

    def phi_copy(d):
        return pltpu.make_async_remote_copy(
            src_ref=phi_ref.at[ahead(d)],
            dst_ref=table_ref.at[slab],
            send_sem=phi_send.at[d],
            recv_sem=phi_recv.at[d],
            device_id=(ahead(d), grp),
            device_id_type=MESH,
        )

    part_copies = [
        pltpu.make_async_remote_copy(
            src_ref=near,
            dst_ref=far,
            send_sem=part_send.at[n],
            recv_sem=part_recv.at[n],
            device_id=below,
            device_id_type=MESH,
        )
        for n, (near, far) in enumerate(zip(parts, far_parts))
    ]
    back_copy = pltpu.make_async_remote_copy(
        src_ref=sent_ref,
        dst_ref=back_ref,
        send_sem=back_send,
        recv_sem=back_recv,
        device_id=above,
        device_id_type=MESH,
    )

    def each(action):
        def step(d, _):
            action(d)
            return 0

        lax.fori_loop(1, slabs, step, 0)

    each(lambda d: member_copy(d).start())
    for copy in part_copies:
        copy.start()

    own_part(early, later, *own)

    member_ref[slab] = group_ref[slab]
    each(lambda d: member_copy(d).wait())
    phi_part(member_ref, phi_ref, energy_ref, phi_target_ref, phi_source_ref)
    each(lambda d: phi_copy(d).start())
    table_ref[slab] = phi_ref[slab]

    for copy in part_copies:
        copy.wait()
    fill(far_parts, plane_ref, None, far_ref, 1.0)
    cross_part(list_ref, dens_ref, column_ref, sent_ref, left_ref, far_ref, near_even_ref, near_odd_ref)
    back_copy.start()

    own_part(later, blocks, *own)
    each(lambda d: phi_copy(d).wait())
    back_copy.wait()


def block_of(parts, i):
    place_ref, mass_ref, size_ref = parts
    row = lax.broadcasted_iota(jnp.int32, (8, TILE), 0)
    block = jnp.broadcast_to(size_ref[pl.ds(i, 1), :], (8, TILE))
    block = jnp.where(row == 3, mass_ref[pl.ds(i, 1), :], block)
    for axis in range(3):
        block = jnp.where(row == axis, place_ref[axis, pl.ds(i, 1), :], block)
    return block


def pick_kernel(place_ref, weight_ref, size_ref, count_ref, owner_ref, out_ref):
    parts = (place_ref, weight_ref, size_ref)
    blocks = weight_ref.shape[0]
    row = lax.broadcasted_iota(jnp.int32, (8, TILE), 0)
    lane = lax.broadcasted_iota(jnp.int32, (8, TILE), 1)

    def step(k, start):
        count = count_ref[0, k]
        block = jnp.minimum(start // TILE, blocks - 1)
        shift = start % TILE
        after = jnp.minimum(block + 1, blocks - 1)
        first = block_of(parts, block)
        second = block_of(parts, after)
        mixed = pltpu.roll(jnp.where(lane >= shift, first, second), (TILE - shift) % TILE, 1)
        out_ref[owner_ref[0, k]] = jnp.where((row == 3) & (lane >= count), 0.0, mixed)
        return start + count

    lax.fori_loop(0, count_ref.shape[1], step, jnp.int32(0), unroll=8)


def phi_part(member_ref, phi_ref, energy_ref, target_ref, source_ref):
    slabs = member_ref.shape[0]
    group = math.gcd(slabs, 8)

    def fill(i, _):
        particles = member_ref[i]
        row, coords, norm = centred(particles, 0.0)
        size = particles[4:5]
        norm = norm + 0.125 * size * size
        base = pl.multiple_of(i * TILE, TILE)
        source_ref[:, pl.ds(base, TILE)] = right_rows(
            jnp.where(row < 3, coords, jnp.where(row == 3, norm, jnp.where(row == 4, 1.0, 0.0)))
        )
        target_ref[:, pl.ds(base, TILE)] = left_rows(
            jnp.where(row < 3, -2.0 * coords, jnp.where(row == 3, 1.0, jnp.where(row == 4, norm, 0.0)))
        )
        return 0

    lax.fori_loop(0, slabs, fill, 0)

    def step(i, energy):
        target = target_ref[:, pl.ds(pl.multiple_of(i * TILE, TILE), TILE)]

        def inner(j, total):
            for n in range(group):
                base = pl.multiple_of((j * group + n) * TILE, TILE)
                pairs = pair_dot(target, source_ref[:, pl.ds(base, TILE)])
                total = total + lax.rsqrt(pairs) * member_ref[j * group + n, 3:4, :]
            return total

        total = lax.fori_loop(0, slabs // group, inner, jnp.zeros((TILE, TILE), F32), unroll=slabs == group)
        mass = member_ref[i, 3:4, :]
        size = member_ref[i, 4:5, :]
        phi = mass * (2.0 / size) - jnp.sum(total.T, axis=0, keepdims=True)
        phi_ref[i] = phi
        return energy + mass * phi

    energy = lax.fori_loop(0, slabs, step, jnp.zeros((1, TILE), F32), unroll=4 if slabs == group else 1)
    energy_ref[...] = 0.5 * jnp.sum(energy, axis=1, keepdims=True)


def final_kernel(mass_ref, dens_ref, back_ref, table_ref, count_ref, owner_ref, out_ref, pot_ref, work_ref):
    out_ref[...] = (dens_ref[...] + back_ref[...]) * (DENSITY_SCALE / mass_ref[...])
    work_ref[...] = jnp.zeros_like(work_ref)
    lane = lax.broadcasted_iota(jnp.int32, (1, TILE), 1)

    def step(k, start):
        count = count_ref[0, k]
        block = start // TILE
        shift = start % TILE
        value = table_ref[owner_ref[0, k]]
        value = pltpu.roll(jnp.where(lane < count, value, 0.0), shift, 1)
        work_ref[pl.ds(block, 1), :] += jnp.where(lane >= shift, value, 0.0)
        work_ref[pl.ds(block + 1, 1), :] += jnp.where(lane < shift, value, 0.0)
        return start + count

    lax.fori_loop(0, count_ref.shape[1], step, jnp.int32(0), unroll=8)
    pot_ref[...] = work_ref[: pot_ref.shape[0], :]


def per_device(positions, masses, smoothing, block_lists, block_counts, group_owner):
    row_count = masses.shape[1]
    blocks = row_count // TILE
    groups = block_counts.shape[1]
    slabs = lax.axis_size("slab")
    grps = lax.axis_size("grp")
    particles = (
        positions[0].reshape(3, blocks, TILE),
        masses.reshape(blocks, TILE),
        smoothing.reshape(blocks, TILE),
    )
    outgoing = pl.pallas_call(
        pick_kernel,
        out_shape=jax.ShapeDtypeStruct((groups, 8, TILE), F32),
        in_specs=[VMEM, VMEM, VMEM, SMEM, SMEM],
        out_specs=VMEM,
    )(*particles, block_counts, group_owner)

    grid_shape = jax.ShapeDtypeStruct((blocks, TILE), F32)
    row_shape = jax.ShapeDtypeStruct((slabs, 1, TILE), F32)
    dma = pltpu.SemaphoreType.DMA
    density, table, back, energy = pl.pallas_call(
        functools.partial(main_kernel, slabs, grps),
        out_shape=(grid_shape, row_shape, grid_shape, jax.ShapeDtypeStruct((1, 1), F32)),
        in_specs=[VMEM, VMEM, VMEM, VMEM, SMEM],
        out_specs=(VMEM, VMEM, VMEM, VMEM),
        scratch_shapes=[
            pltpu.VMEM((3, blocks, TILE), F32),
            pltpu.VMEM((blocks, TILE), F32),
            pltpu.VMEM((blocks, TILE), F32),
            pltpu.VMEM((slabs, 8, TILE), F32),
            pltpu.VMEM((slabs, 1, TILE), F32),
            pltpu.VMEM((KX * blocks, TILE), F32),
            pltpu.VMEM((blocks, TILE), F32),
            pltpu.VMEM((blocks, TILE, DEPTH), HALF),
            pltpu.VMEM((blocks, DEPTH, 3 * TILE), HALF),
            pltpu.VMEM((blocks, DEPTH, 3 * TILE), HALF),
            pltpu.VMEM((KO * TILE, 3 * TILE), F32),
            pltpu.VMEM((KO * TILE, 3 * TILE), F32),
            pltpu.VMEM((KX * TILE, 3 * TILE), F32),
            pltpu.VMEM((KX * TILE, 3 * TILE), F32),
            pltpu.VMEM((48, slabs * TILE), HALF),
            pltpu.VMEM((48, slabs * TILE), HALF),
            pltpu.VMEM((PLANES, blocks, TILE), F32),
            dma((slabs,)),
            dma((slabs,)),
            dma((slabs,)),
            dma((slabs,)),
            dma((3,)),
            dma((3,)),
            dma,
            dma,
        ],
        compiler_params=pltpu.CompilerParams(collective_id=0, has_side_effects=True),
    )(*particles, outgoing, block_lists[0].T)
    density, potential = pl.pallas_call(
        final_kernel,
        out_shape=(grid_shape, grid_shape),
        in_specs=[VMEM, VMEM, VMEM, VMEM, SMEM, SMEM],
        out_specs=(VMEM, VMEM),
        scratch_shapes=[pltpu.VMEM((blocks + 8, TILE), F32)],
    )(particles[1], density, back, table, block_counts, group_owner)
    return (density.reshape(1, row_count), potential.reshape(1, row_count), energy)


def solution(mesh):
    placed = (
        P(("slab", "grp"), None, None),
        P(("slab", "grp"), None),
        P(("slab", "grp"), None),
        P(("slab", "grp"), None, None),
        P(("slab", "grp"), None),
        P("grp", None),
    )
    return jax.shard_map(
        per_device,
        mesh=mesh,
        in_specs=placed,
        out_specs=(P(("slab", "grp"), None), P(("slab", "grp"), None), P("grp", "slab")),
        check_vma=False,
    )
```

```python
import functools
import math

import jax
import jax.numpy as jnp
from jax import lax
from jax.experimental import pallas as pl
from jax.experimental.pallas import tpu as pltpu
from jax.sharding import PartitionSpec as P

TILE = 128
KX = 2
KO = 4
F32 = jnp.float32
HALF = jnp.bfloat16
DEPTH = 64
LOT = 8

DENSITY_SCALE = 21.0 / (256.0 * math.pi) / 16.0

VMEM = pl.BlockSpec(memory_space=pltpu.VMEM)
MESH = pl.DeviceIdType.MESH
SMEM = pl.BlockSpec(memory_space=pltpu.SMEM)


def split3(a):
    high = a.astype(HALF).astype(F32)
    rest = a - high
    mid = rest.astype(HALF).astype(F32)
    return high, mid, rest - mid


def left_six(a):
    high, mid, low = split3(a)
    return [high, high, mid, high, low, mid]


def right_six(a):
    high, mid, low = split3(a)
    return [high, mid, high, low, high, mid]


def left_rows(a):
    return jnp.concatenate(left_six(a), axis=0).astype(HALF)


def right_rows(a):
    return jnp.concatenate(right_six(a), axis=0).astype(HALF)


def centred(particles, lift):
    row = lax.broadcasted_iota(jnp.int32, particles.shape, 0)
    shift = jnp.where(row == 0, lift - 0.5, jnp.where(row < 3, -0.5, 0.0))
    coords = jnp.where(row < 3, particles + shift, 0.0)
    norm = jnp.sum(coords * coords, axis=0, keepdims=True)
    return row, coords, norm


FACTORS = 8
NORM, SIZE, PLANES = 8, 11, 14


def fill_planes(parts, plane_ref, lift):
    place_ref, mass_ref, size_ref = parts

    def step(i, _):
        rows = pl.ds(pl.multiple_of(i * LOT, LOT), LOT)
        coords = [place_ref[axis, rows, :] + ((lift if axis == 0 else 0.0) - 0.5) for axis in range(3)]
        norm = coords[0] * coords[0] + coords[1] * coords[1] + coords[2] * coords[2]
        size = size_ref[rows, :]
        planes = coords + [lax.rsqrt(mass_ref[rows, :])]
        for _ in range(4):
            planes.append(planes[-1] * size)
        planes += list(split3(norm)) + list(split3(size))
        for n, plane in enumerate(planes):
            plane_ref[n, rows, :] = plane
        return 0

    lax.fori_loop(0, mass_ref.shape[0] // LOT, step, 0, unroll=2)


def by_row(values):
    row = lax.broadcasted_iota(jnp.int32, (8, TILE), 0)
    block = jnp.broadcast_to(values[0], (8, TILE))
    for n, value in enumerate(values[1:]):
        block = jnp.where(row == n + 1, value, block)
    return block


def fill(parts, plane_ref, left_ref, right_ref, lift):
    fill_planes(parts, plane_ref, lift)
    row = lax.broadcasted_iota(jnp.int32, (8, TILE), 0)
    zero = jnp.zeros((8, TILE), F32)

    def step(i, _):
        plane = [plane_ref[n, pl.ds(i, 1), :] for n in range(PLANES)]
        coords, powers, norm, size = plane[:3], plane[3:8], plane[NORM:SIZE], plane[SIZE:]
        if left_ref is not None:
            high, mid, low = split3(by_row(coords + powers[::-1]))
            rest = by_row(norm + [1.0, 1.0, 1.0] + size[:2])
            last = jnp.where(row == 0, size[2], 0.0)
            left_ref[i] = jnp.concatenate([high, high, high, mid, mid, low, rest, last], axis=0).T.astype(HALF)
        scale = by_row([-8.0, -8.0, -8.0, 0.0625, 0.25, 0.375, 0.25, 0.0625])
        parts3 = split3(scale * by_row(coords + powers))
        near = [jnp.where(row < 3, part, 0.0) for part in parts3]
        far = [jnp.where(row < 3, 0.0, part) for part in parts3]
        order = (0, 1, 2, 0, 1, 0)
        rest = by_row([4.0, 4.0, 4.0] + [4.0 * part for part in norm] + [0.0, 0.0])
        wide = by_row([0.0, 0.0, 0.0] + [2.0 * part for part in size] + [2.0, 2.0])
        last = jnp.where(row == 0, 2.0, 0.0)
        columns = (
            [near[n] for n in order] + [rest, zero],
            [zero] * 6 + [wide, last],
            [far[n] for n in order] + [zero, zero],
        )
        for m, column in enumerate(columns):
            right_ref[i, :, pl.ds(m * TILE, TILE)] = jnp.concatenate(column, axis=0).astype(HALF)
        return 0

    lax.fori_loop(0, right_ref.shape[0], step, 0, unroll=8)


def pair_dot(left, right, left_dim=0):
    return lax.dot_general(
        left, right, (((left_dim,), (0,)), ((), ())), preferred_element_type=F32
    )


def weights(both_ref, base):
    rows = pl.ds(base, 8)
    squared = jnp.maximum(both_ref[rows, :TILE], 1e-30)
    reach = both_ref[rows, TILE : 2 * TILE]
    near = jnp.maximum(reach - squared * lax.rsqrt(squared), 0.0)
    a = near * lax.rsqrt(both_ref[rows, 2 * TILE : 3 * TILE])
    a = a * a
    return (a * a) * (1.25 * reach - near)


def sweep(first, last, end, fetch, use, even_ref, odd_ref, unroll):
    def step(i, _):
        b = first + 2 * i
        fetch(b + 1, odd_ref)
        use(b, even_ref)
        fetch(jnp.minimum(b + 2, end - 1), even_ref)
        use(b + 1, odd_ref)
        return 0

    lax.fori_loop(0, (last - first) // 2, step, 0, unroll=unroll)


def steps_of(first, last, most):
    return math.gcd((last - first) // 2, most)


def own_part(first, last, list_ref, dens_ref, left_ref, right_ref, even_ref, odd_ref):
    def fetch(b, both_ref):
        right = right_ref[b]
        for k in range(KO):
            both_ref[pl.ds(k * TILE, TILE), :] = pair_dot(left_ref[list_ref[KX + k, b]], right, 1)

    def use(b, both_ref):
        total = jnp.zeros((8, TILE), F32)
        for base in range(0, KO * TILE, 8):
            total = total + weights(both_ref, base)
        dens_ref[pl.ds(b, 1), :] += jnp.sum(total, axis=0, keepdims=True)

    if first == 0:
        fetch(0, even_ref)
    sweep(first, last, left_ref.shape[0], fetch, use, even_ref, odd_ref, steps_of(first, last, 12 if (last - first) % 3 == 0 else 8))


def cross_part(list_ref, dens_ref, column_ref, back_ref, left_ref, right_ref, even_ref, odd_ref):
    blocks = left_ref.shape[0]

    def fetch(b, both_ref):
        left = left_ref[b]
        for k in range(KX):
            both_ref[pl.ds(k * TILE, TILE), :] = pair_dot(left, right_ref[list_ref[KX + KO + k, b]], 1)

    def use(b, both_ref):
        column = [jnp.zeros((8, TILE), F32)] * KX
        total = []
        for base in range(0, TILE, 8):
            values = [weights(both_ref, k * TILE + base) for k in range(KX)]
            column = [old + value for old, value in zip(column, values)]
            total.append(sum(values))
        for k in range(KX):
            column_ref[pl.ds(KX * b + k, 1), :] = jnp.sum(column[k], axis=0, keepdims=True)
        total = jnp.concatenate(total, axis=0)
        dens_ref[pl.ds(b, 1), :] += jnp.sum(total.T, axis=0, keepdims=True)

    fetch(0, even_ref)
    sweep(0, blocks, blocks, fetch, use, even_ref, odd_ref, steps_of(0, blocks, 8))

    lane = lax.broadcasted_iota(jnp.int32, (1, KX * blocks), 1)

    def name(b, row):
        for k in range(KX):
            row = jnp.where(lane == KX * b + k, list_ref[KX + KO + k, b], row)
        return row

    named = lax.fori_loop(0, blocks, name, jnp.zeros((1, KX * blocks), jnp.int32), unroll=8)
    block = lax.broadcasted_iota(jnp.int32, (blocks, KX * blocks), 0)
    chosen = jnp.where(block == named, 1.0, 0.0).astype(HALF)
    high, mid, low = split3(column_ref[...])
    back_ref[...] = sum(
        jnp.dot(chosen, part.astype(HALF), preferred_element_type=F32) for part in (low, mid, high)
    )


def main_kernel(
    slabs,
    grps,
    place_ref,
    weight_ref,
    size_ref,
    list_ref,
    count_ref,
    owner_ref,
    dens_ref,
    table_ref,
    back_ref,
    energy_ref,
    far_place_ref,
    far_weight_ref,
    far_size_ref,
    group_ref,
    member_ref,
    phi_ref,
    column_ref,
    sent_ref,
    left_ref,
    right_ref,
    far_ref,
    even_ref,
    odd_ref,
    near_even_ref,
    near_odd_ref,
    phi_target_ref,
    phi_source_ref,
    plane_ref,
    member_send,
    member_recv,
    phi_send,
    phi_recv,
    part_send,
    part_recv,
    back_send,
    back_recv,
):
    slab = lax.axis_index("slab")
    grp = lax.axis_index("grp")
    count = slabs * grps
    here = slab * grps + grp

    def place(index):
        return (index // grps, lax.rem(index, grps))

    above = place(lax.rem(here + 1, count))
    below = place(lax.rem(here + count - 1, count))

    def ahead(d):
        return lax.rem(slab + d, slabs)

    barrier = pltpu.get_barrier_semaphore()
    for other in (above, below):
        pl.semaphore_signal(barrier, inc=1, device_id=other, device_id_type=MESH)

    def greet(d, _):
        pl.semaphore_signal(barrier, inc=1, device_id=(ahead(d), grp), device_id_type=MESH)
        return 0

    lax.fori_loop(1, slabs, greet, 0)
    parts = (place_ref, weight_ref, size_ref)
    far_parts = (far_place_ref, far_weight_ref, far_size_ref)
    blocks = dens_ref.shape[0]
    early = blocks // 16 * 2
    later = blocks // 4 * 2
    own = (list_ref, dens_ref, left_ref, right_ref, even_ref, odd_ref)
    dens_ref[...] = jnp.zeros_like(dens_ref)
    fill(parts, plane_ref, left_ref, right_ref, 0.0)
    pick_groups(parts, count_ref, owner_ref, group_ref)
    own_part(0, early, *own)
    pl.semaphore_wait(barrier, slabs + 1)

    def member_copy(d):
        return pltpu.make_async_remote_copy(
            src_ref=group_ref.at[ahead(d)],
            dst_ref=member_ref.at[slab],
            send_sem=member_send.at[d],
            recv_sem=member_recv.at[d],
            device_id=(ahead(d), grp),
            device_id_type=MESH,
        )

    def phi_copy(d):
        return pltpu.make_async_remote_copy(
            src_ref=phi_ref.at[ahead(d)],
            dst_ref=table_ref.at[slab],
            send_sem=phi_send.at[d],
            recv_sem=phi_recv.at[d],
            device_id=(ahead(d), grp),
            device_id_type=MESH,
        )

    part_copies = [
        pltpu.make_async_remote_copy(
            src_ref=near,
            dst_ref=far,
            send_sem=part_send.at[n],
            recv_sem=part_recv.at[n],
            device_id=below,
            device_id_type=MESH,
        )
        for n, (near, far) in enumerate(zip(parts, far_parts))
    ]
    back_copy = pltpu.make_async_remote_copy(
        src_ref=sent_ref,
        dst_ref=back_ref,
        send_sem=back_send,
        recv_sem=back_recv,
        device_id=above,
        device_id_type=MESH,
    )

    def each(action):
        def step(d, _):
            action(d)
            return 0

        lax.fori_loop(1, slabs, step, 0)

    each(lambda d: member_copy(d).start())
    for copy in part_copies:
        copy.start()

    own_part(early, later, *own)

    for copy in part_copies:
        copy.wait()
    fill(far_parts, plane_ref, None, far_ref, 1.0)
    cross_part(list_ref, dens_ref, column_ref, sent_ref, left_ref, far_ref, near_even_ref, near_odd_ref)
    back_copy.start()

    member_ref[slab] = group_ref[slab]
    each(lambda d: member_copy(d).wait())
    phi_part(member_ref, phi_ref, energy_ref, phi_target_ref, phi_source_ref)
    each(lambda d: phi_copy(d).start())
    table_ref[slab] = phi_ref[slab]

    own_part(later, blocks, *own)
    each(lambda d: phi_copy(d).wait())
    back_copy.wait()


def block_of(parts, i):
    place_ref, mass_ref, size_ref = parts
    row = lax.broadcasted_iota(jnp.int32, (8, TILE), 0)
    block = jnp.broadcast_to(size_ref[pl.ds(i, 1), :], (8, TILE))
    block = jnp.where(row == 3, mass_ref[pl.ds(i, 1), :], block)
    for axis in range(3):
        block = jnp.where(row == axis, place_ref[axis, pl.ds(i, 1), :], block)
    return block


def pick_groups(parts, count_ref, owner_ref, group_ref):
    blocks = parts[1].shape[0]
    row = lax.broadcasted_iota(jnp.int32, (8, TILE), 0)
    lane = lax.broadcasted_iota(jnp.int32, (8, TILE), 1)
    slot = lax.broadcasted_iota(jnp.int32, group_ref.shape, 0)

    def step(k, start):
        count = count_ref[0, k]
        block = jnp.minimum(start // TILE, blocks - 1)
        shift = start % TILE
        first = block_of(parts, block)
        second = block_of(parts, jnp.minimum(block + 1, blocks - 1))
        mixed = pltpu.roll(jnp.where(lane >= shift, first, second), (TILE - shift) % TILE, 1)
        mixed = jnp.where((row == 3) & (lane >= count), 0.0, mixed)
        group_ref[...] = jnp.where(slot == owner_ref[0, k], mixed, group_ref[...])
        return start + count

    group_ref[...] = jnp.zeros_like(group_ref)
    groups = count_ref.shape[1]
    lax.fori_loop(0, groups, step, jnp.int32(0), unroll=math.gcd(groups, 8))


def phi_part(member_ref, phi_ref, energy_ref, target_ref, source_ref):
    slabs = member_ref.shape[0]
    group = math.gcd(slabs, 8)

    def fill(i, _):
        particles = member_ref[i]
        row, coords, norm = centred(particles, 0.0)
        size = particles[4:5]
        norm = norm + 0.125 * size * size
        base = pl.multiple_of(i * TILE, TILE)
        source_ref[:, pl.ds(base, TILE)] = right_rows(
            jnp.where(row < 3, coords, jnp.where(row == 3, norm, jnp.where(row == 4, 1.0, 0.0)))
        )
        target_ref[:, pl.ds(base, TILE)] = left_rows(
            jnp.where(row < 3, -2.0 * coords, jnp.where(row == 3, 1.0, jnp.where(row == 4, norm, 0.0)))
        )
        return 0

    lax.fori_loop(0, slabs, fill, 0)

    def step(i, energy):
        target = target_ref[:, pl.ds(pl.multiple_of(i * TILE, TILE), TILE)]

        def inner(j, total):
            for n in range(group):
                base = pl.multiple_of((j * group + n) * TILE, TILE)
                pairs = pair_dot(target, source_ref[:, pl.ds(base, TILE)])
                total = total + lax.rsqrt(pairs) * member_ref[j * group + n, 3:4, :]
            return total

        total = lax.fori_loop(0, slabs // group, inner, jnp.zeros((TILE, TILE), F32), unroll=slabs == group)
        mass = member_ref[i, 3:4, :]
        size = member_ref[i, 4:5, :]
        phi = mass * (2.0 / size) - jnp.sum(total.T, axis=0, keepdims=True)
        phi_ref[i] = phi
        return energy + mass * phi

    energy = lax.fori_loop(0, slabs, step, jnp.zeros((1, TILE), F32), unroll=4 if slabs == group else 1)
    energy_ref[...] = 0.5 * jnp.sum(energy, axis=1, keepdims=True)


def final_kernel(mass_ref, dens_ref, back_ref, table_ref, energy_ref, count_ref, owner_ref, out_ref, pot_ref, total_ref, work_ref):
    total_ref[...] = energy_ref[...]
    out_ref[...] = (dens_ref[...] + back_ref[...]) * (DENSITY_SCALE / mass_ref[...])
    work_ref[...] = jnp.zeros_like(work_ref)
    lane = lax.broadcasted_iota(jnp.int32, (1, TILE), 1)

    def step(k, start):
        count = count_ref[0, k]
        block = start // TILE
        shift = start % TILE
        value = table_ref[owner_ref[0, k]]
        value = pltpu.roll(jnp.where(lane < count, value, 0.0), shift, 1)
        work_ref[pl.ds(block, 1), :] += jnp.where(lane >= shift, value, 0.0)
        work_ref[pl.ds(block + 1, 1), :] += jnp.where(lane < shift, value, 0.0)
        return start + count

    lax.fori_loop(0, count_ref.shape[1], step, jnp.int32(0), unroll=8)
    pot_ref[...] = work_ref[: pot_ref.shape[0], :]


def per_device(positions, masses, smoothing, block_lists, block_counts, group_owner):
    row_count = masses.shape[1]
    blocks = row_count // TILE
    slabs = lax.axis_size("slab")
    grps = lax.axis_size("grp")
    particles = (
        positions[0].reshape(3, blocks, TILE),
        masses.reshape(blocks, TILE),
        smoothing.reshape(blocks, TILE),
    )
    grid_shape = jax.ShapeDtypeStruct((blocks, TILE), F32)
    row_shape = jax.ShapeDtypeStruct((slabs, 1, TILE), F32)
    dma = pltpu.SemaphoreType.DMA
    density, table, back, energy = pl.pallas_call(
        functools.partial(main_kernel, slabs, grps),
        out_shape=(grid_shape, row_shape, grid_shape, jax.ShapeDtypeStruct((1, 1), F32)),
        in_specs=[VMEM, VMEM, VMEM, SMEM, SMEM, SMEM],
        out_specs=(VMEM, VMEM, VMEM, VMEM),
        scratch_shapes=[
            pltpu.VMEM((3, blocks, TILE), F32),
            pltpu.VMEM((blocks, TILE), F32),
            pltpu.VMEM((blocks, TILE), F32),
            pltpu.VMEM((slabs, 8, TILE), F32),
            pltpu.VMEM((slabs, 8, TILE), F32),
            pltpu.VMEM((slabs, 1, TILE), F32),
            pltpu.VMEM((KX * blocks, TILE), F32),
            pltpu.VMEM((blocks, TILE), F32),
            pltpu.VMEM((blocks, TILE, DEPTH), HALF),
            pltpu.VMEM((blocks, DEPTH, 3 * TILE), HALF),
            pltpu.VMEM((blocks, DEPTH, 3 * TILE), HALF),
            pltpu.VMEM((KO * TILE, 3 * TILE), F32),
            pltpu.VMEM((KO * TILE, 3 * TILE), F32),
            pltpu.VMEM((KX * TILE, 3 * TILE), F32),
            pltpu.VMEM((KX * TILE, 3 * TILE), F32),
            pltpu.VMEM((48, slabs * TILE), HALF),
            pltpu.VMEM((48, slabs * TILE), HALF),
            pltpu.VMEM((PLANES, blocks, TILE), F32),
            dma((slabs,)),
            dma((slabs,)),
            dma((slabs,)),
            dma((slabs,)),
            dma((3,)),
            dma((3,)),
            dma,
            dma,
        ],
        compiler_params=pltpu.CompilerParams(collective_id=0, has_side_effects=True),
    )(*particles, block_lists[0].T, block_counts, group_owner)
    density, potential, energy = pl.pallas_call(
        final_kernel,
        out_shape=(grid_shape, grid_shape, jax.ShapeDtypeStruct((1, 1), F32)),
        in_specs=[VMEM, VMEM, VMEM, VMEM, VMEM, SMEM, SMEM],
        out_specs=(VMEM, VMEM, VMEM),
        scratch_shapes=[pltpu.VMEM((blocks + 8, TILE), F32)],
    )(particles[1], density, back, table, energy, block_counts, group_owner)
    return (density.reshape(1, row_count), potential.reshape(1, row_count), energy)


def solution(mesh):
    placed = (
        P(("slab", "grp"), None, None),
        P(("slab", "grp"), None),
        P(("slab", "grp"), None),
        P(("slab", "grp"), None, None),
        P(("slab", "grp"), None),
        P("grp", None),
    )
    return jax.shard_map(
        per_device,
        mesh=mesh,
        in_specs=placed,
        out_specs=(P(("slab", "grp"), None), P(("slab", "grp"), None), P("grp", "slab")),
        check_vma=False,
    )
```

```python
import functools
import math

import jax
import jax.numpy as jnp
from jax import lax
from jax.experimental import pallas as pl
from jax.experimental.pallas import tpu as pltpu
from jax.sharding import PartitionSpec as P

TILE = 128
KX = 2
KO = 4
F32 = jnp.float32
HALF = jnp.bfloat16
DEPTH = 64
LOT = 8

DENSITY_SCALE = 21.0 / (256.0 * math.pi) / 16.0

VMEM = pl.BlockSpec(memory_space=pltpu.VMEM)
MESH = pl.DeviceIdType.MESH
SMEM = pl.BlockSpec(memory_space=pltpu.SMEM)


def split3(a):
    high = a.astype(HALF).astype(F32)
    rest = a - high
    mid = rest.astype(HALF).astype(F32)
    return high, mid, rest - mid


def left_six(a):
    high, mid, low = split3(a)
    return [high, high, mid, high, low, mid]


def right_six(a):
    high, mid, low = split3(a)
    return [high, mid, high, low, high, mid]


def left_rows(a):
    return jnp.concatenate(left_six(a), axis=0).astype(HALF)


def right_rows(a):
    return jnp.concatenate(right_six(a), axis=0).astype(HALF)


def centred(particles, lift):
    row = lax.broadcasted_iota(jnp.int32, particles.shape, 0)
    shift = jnp.where(row == 0, lift - 0.5, jnp.where(row < 3, -0.5, 0.0))
    coords = jnp.where(row < 3, particles + shift, 0.0)
    norm = jnp.sum(coords * coords, axis=0, keepdims=True)
    return row, coords, norm


FACTORS = 8
NORM, SIZE, PLANES = 8, 11, 14


def fill_planes(parts, plane_ref, lift):
    place_ref, mass_ref, size_ref = parts

    def step(i, _):
        rows = pl.ds(pl.multiple_of(i * LOT, LOT), LOT)
        coords = [place_ref[axis, rows, :] + ((lift if axis == 0 else 0.0) - 0.5) for axis in range(3)]
        norm = coords[0] * coords[0] + coords[1] * coords[1] + coords[2] * coords[2]
        size = size_ref[rows, :]
        planes = coords + [lax.rsqrt(mass_ref[rows, :])]
        for _ in range(4):
            planes.append(planes[-1] * size)
        planes += list(split3(norm)) + list(split3(size))
        for n, plane in enumerate(planes):
            plane_ref[n, rows, :] = plane
        return 0

    lax.fori_loop(0, mass_ref.shape[0] // LOT, step, 0, unroll=2)


def by_row(values):
    row = lax.broadcasted_iota(jnp.int32, (8, TILE), 0)
    block = jnp.broadcast_to(values[0], (8, TILE))
    for n, value in enumerate(values[1:]):
        block = jnp.where(row == n + 1, value, block)
    return block


def fill(parts, plane_ref, left_ref, right_ref, lift):
    fill_planes(parts, plane_ref, lift)
    row = lax.broadcasted_iota(jnp.int32, (8, TILE), 0)
    zero = jnp.zeros((8, TILE), F32)

    def step(i, _):
        plane = [plane_ref[n, pl.ds(i, 1), :] for n in range(PLANES)]
        coords, powers, norm, size = plane[:3], plane[3:8], plane[NORM:SIZE], plane[SIZE:]
        high, mid, low = split3(by_row(coords + powers[::-1]))
        rest = by_row(norm + [1.0, 1.0, 1.0] + size[:2])
        last = jnp.where(row == 0, size[2], 0.0)
        left_ref[i] = jnp.concatenate([high, high, high, mid, mid, low, rest, last], axis=0).T.astype(HALF)
        if right_ref is not None:
            scale = by_row([-8.0, -8.0, -8.0, 0.0625, 0.25, 0.375, 0.25, 0.0625])
            parts3 = split3(scale * by_row(coords + powers))
            near = [jnp.where(row < 3, part, 0.0) for part in parts3]
            far = [jnp.where(row < 3, 0.0, part) for part in parts3]
            order = (0, 1, 2, 0, 1, 0)
            rest = by_row([4.0, 4.0, 4.0] + [4.0 * part for part in norm] + [0.0, 0.0])
            wide = by_row([0.0, 0.0, 0.0] + [2.0 * part for part in size] + [2.0, 2.0])
            last = jnp.where(row == 0, 2.0, 0.0)
            columns = (
                [near[n] for n in order] + [rest, zero],
                [zero] * 6 + [wide, last],
                [far[n] for n in order] + [zero, zero],
            )
            for m, column in enumerate(columns):
                right_ref[i, :, pl.ds(m * TILE, TILE)] = jnp.concatenate(column, axis=0).astype(HALF)
        return 0

    lax.fori_loop(0, left_ref.shape[0], step, 0, unroll=8)


def pair_dot(left, right, left_dim=0):
    return lax.dot_general(
        left, right, (((left_dim,), (0,)), ((), ())), preferred_element_type=F32
    )


def weights(both_ref, base):
    rows = pl.ds(base, 8)
    squared = jnp.maximum(both_ref[rows, :TILE], 1e-30)
    reach = both_ref[rows, TILE : 2 * TILE]
    near = jnp.maximum(reach - squared * lax.rsqrt(squared), 0.0)
    a = near * lax.rsqrt(both_ref[rows, 2 * TILE : 3 * TILE])
    a = a * a
    return (a * a) * (1.25 * reach - near)


def sweep(first, last, end, fetch, use, even_ref, odd_ref, unroll):
    def step(i, _):
        b = first + 2 * i
        fetch(b + 1, odd_ref)
        use(b, even_ref)
        fetch(jnp.minimum(b + 2, end - 1), even_ref)
        use(b + 1, odd_ref)
        return 0

    lax.fori_loop(0, (last - first) // 2, step, 0, unroll=unroll)


def steps_of(first, last, most):
    return math.gcd((last - first) // 2, most)


def own_part(first, last, list_ref, dens_ref, left_ref, right_ref, even_ref, odd_ref):
    def fetch(b, both_ref):
        right = right_ref[b]
        for k in range(KO):
            both_ref[pl.ds(k * TILE, TILE), :] = pair_dot(left_ref[list_ref[KX + k, b]], right, 1)

    def use(b, both_ref):
        total = jnp.zeros((8, TILE), F32)
        for base in range(0, KO * TILE, 8):
            total = total + weights(both_ref, base)
        dens_ref[pl.ds(b, 1), :] += jnp.sum(total, axis=0, keepdims=True)

    if first == 0:
        fetch(0, even_ref)
    sweep(first, last, left_ref.shape[0], fetch, use, even_ref, odd_ref, steps_of(first, last, 8))


def cross_part(list_ref, dens_ref, column_ref, back_ref, far_ref, right_ref, even_ref, odd_ref):
    blocks = far_ref.shape[0]

    def fetch(b, both_ref):
        left = jnp.concatenate([far_ref[list_ref[KX + KO + k, b]] for k in range(KX)], axis=0)
        both_ref[...] = pair_dot(left, right_ref[b], 1)

    def use(b, both_ref):
        total = jnp.zeros((8, TILE), F32)
        for k in range(KX):
            values = [weights(both_ref, k * TILE + base) for base in range(0, TILE, 8)]
            for value in values:
                total = total + value
            column = jnp.concatenate(values, axis=0).T
            column_ref[pl.ds(KX * b + k, 1), :] = jnp.sum(column, axis=0, keepdims=True)
        dens_ref[pl.ds(b, 1), :] += jnp.sum(total, axis=0, keepdims=True)

    fetch(0, even_ref)
    sweep(0, blocks, blocks, fetch, use, even_ref, odd_ref, steps_of(0, blocks, 8))

    lane = lax.broadcasted_iota(jnp.int32, (1, KX * blocks), 1)

    def name(b, row):
        for k in range(KX):
            row = jnp.where(lane == KX * b + k, list_ref[KX + KO + k, b], row)
        return row

    named = lax.fori_loop(0, blocks, name, jnp.zeros((1, KX * blocks), jnp.int32), unroll=8)
    block = lax.broadcasted_iota(jnp.int32, (blocks, KX * blocks), 0)
    chosen = jnp.where(block == named, 1.0, 0.0).astype(HALF)
    high, mid, low = split3(column_ref[...])
    back_ref[...] = sum(
        jnp.dot(chosen, part.astype(HALF), preferred_element_type=F32) for part in (low, mid, high)
    )


def main_kernel(
    slabs,
    grps,
    place_ref,
    weight_ref,
    size_ref,
    list_ref,
    count_ref,
    owner_ref,
    dens_ref,
    table_ref,
    back_ref,
    energy_ref,
    far_place_ref,
    far_weight_ref,
    far_size_ref,
    group_ref,
    member_ref,
    phi_ref,
    column_ref,
    sent_ref,
    left_ref,
    right_ref,
    far_ref,
    even_ref,
    odd_ref,
    near_even_ref,
    near_odd_ref,
    phi_target_ref,
    phi_source_ref,
    plane_ref,
    member_send,
    member_recv,
    phi_send,
    phi_recv,
    part_send,
    part_recv,
    back_send,
    back_recv,
):
    slab = lax.axis_index("slab")
    grp = lax.axis_index("grp")
    count = slabs * grps
    here = slab * grps + grp

    def place(index):
        return (index // grps, lax.rem(index, grps))

    above = place(lax.rem(here + 1, count))
    below = place(lax.rem(here + count - 1, count))

    def ahead(d):
        return lax.rem(slab + d, slabs)

    barrier = pltpu.get_barrier_semaphore()
    for other in (above, below):
        pl.semaphore_signal(barrier, inc=1, device_id=other, device_id_type=MESH)

    def greet(d, _):
        pl.semaphore_signal(barrier, inc=1, device_id=(ahead(d), grp), device_id_type=MESH)
        return 0

    lax.fori_loop(1, slabs, greet, 0)
    parts = (place_ref, weight_ref, size_ref)
    far_parts = (far_place_ref, far_weight_ref, far_size_ref)
    blocks = dens_ref.shape[0]
    later = blocks // 4 * 2
    own = (list_ref, dens_ref, left_ref, right_ref, even_ref, odd_ref)
    dens_ref[...] = jnp.zeros_like(dens_ref)
    fill(parts, plane_ref, left_ref, right_ref, 0.0)
    pick_groups(parts, count_ref, owner_ref, group_ref)
    pl.semaphore_wait(barrier, slabs + 1)

    def member_copy(d):
        return pltpu.make_async_remote_copy(
            src_ref=group_ref.at[ahead(d)],
            dst_ref=member_ref.at[slab],
            send_sem=member_send.at[d],
            recv_sem=member_recv.at[d],
            device_id=(ahead(d), grp),
            device_id_type=MESH,
        )

    def phi_copy(d):
        return pltpu.make_async_remote_copy(
            src_ref=phi_ref.at[ahead(d)],
            dst_ref=table_ref.at[slab],
            send_sem=phi_send.at[d],
            recv_sem=phi_recv.at[d],
            device_id=(ahead(d), grp),
            device_id_type=MESH,
        )

    part_copies = [
        pltpu.make_async_remote_copy(
            src_ref=near,
            dst_ref=far,
            send_sem=part_send.at[n],
            recv_sem=part_recv.at[n],
            device_id=below,
            device_id_type=MESH,
        )
        for n, (near, far) in enumerate(zip(parts, far_parts))
    ]
    back_copy = pltpu.make_async_remote_copy(
        src_ref=sent_ref,
        dst_ref=back_ref,
        send_sem=back_send,
        recv_sem=back_recv,
        device_id=above,
        device_id_type=MESH,
    )

    def each(action):
        def step(d, _):
            action(d)
            return 0

        lax.fori_loop(1, slabs, step, 0)

    each(lambda d: member_copy(d).start())
    for copy in part_copies:
        copy.start()

    own_part(0, later, *own)

    for copy in part_copies:
        copy.wait()
    fill(far_parts, plane_ref, far_ref, None, 1.0)
    cross_part(list_ref, dens_ref, column_ref, sent_ref, far_ref, right_ref, near_even_ref, near_odd_ref)
    back_copy.start()

    member_ref[slab] = group_ref[slab]
    each(lambda d: member_copy(d).wait())
    phi_part(member_ref, phi_ref, energy_ref, phi_target_ref, phi_source_ref)
    each(lambda d: phi_copy(d).start())
    table_ref[slab] = phi_ref[slab]

    own_part(later, blocks, *own)
    each(lambda d: phi_copy(d).wait())
    back_copy.wait()


def block_of(parts, i):
    place_ref, mass_ref, size_ref = parts
    row = lax.broadcasted_iota(jnp.int32, (8, TILE), 0)
    block = jnp.broadcast_to(size_ref[pl.ds(i, 1), :], (8, TILE))
    block = jnp.where(row == 3, mass_ref[pl.ds(i, 1), :], block)
    for axis in range(3):
        block = jnp.where(row == axis, place_ref[axis, pl.ds(i, 1), :], block)
    return block


def pick_groups(parts, count_ref, owner_ref, group_ref):
    blocks = parts[1].shape[0]
    row = lax.broadcasted_iota(jnp.int32, (8, TILE), 0)
    lane = lax.broadcasted_iota(jnp.int32, (8, TILE), 1)
    slot = lax.broadcasted_iota(jnp.int32, group_ref.shape, 0)

    def step(k, start):
        count = count_ref[0, k]
        block = jnp.minimum(start // TILE, blocks - 1)
        shift = start % TILE
        first = block_of(parts, block)
        second = block_of(parts, jnp.minimum(block + 1, blocks - 1))
        mixed = pltpu.roll(jnp.where(lane >= shift, first, second), (TILE - shift) % TILE, 1)
        mixed = jnp.where((row == 3) & (lane >= count), 0.0, mixed)
        group_ref[...] = jnp.where(slot == owner_ref[0, k], mixed, group_ref[...])
        return start + count

    group_ref[...] = jnp.zeros_like(group_ref)
    groups = count_ref.shape[1]
    lax.fori_loop(0, groups, step, jnp.int32(0), unroll=math.gcd(groups, 8))


def phi_part(member_ref, phi_ref, energy_ref, target_ref, source_ref):
    slabs = member_ref.shape[0]
    group = math.gcd(slabs, 8)

    def fill(i, _):
        particles = member_ref[i]
        row, coords, norm = centred(particles, 0.0)
        size = particles[4:5]
        norm = norm + 0.125 * size * size
        base = pl.multiple_of(i * TILE, TILE)
        source_ref[:, pl.ds(base, TILE)] = right_rows(
            jnp.where(row < 3, coords, jnp.where(row == 3, norm, jnp.where(row == 4, 1.0, 0.0)))
        )
        target_ref[:, pl.ds(base, TILE)] = left_rows(
            jnp.where(row < 3, -2.0 * coords, jnp.where(row == 3, 1.0, jnp.where(row == 4, norm, 0.0)))
        )
        return 0

    lax.fori_loop(0, slabs, fill, 0)

    def step(i, energy):
        target = target_ref[:, pl.ds(pl.multiple_of(i * TILE, TILE), TILE)]

        def inner(j, total):
            for n in range(group):
                base = pl.multiple_of((j * group + n) * TILE, TILE)
                pairs = pair_dot(target, source_ref[:, pl.ds(base, TILE)])
                total = total + lax.rsqrt(pairs) * member_ref[j * group + n, 3:4, :]
            return total

        total = lax.fori_loop(0, slabs // group, inner, jnp.zeros((TILE, TILE), F32), unroll=slabs == group)
        mass = member_ref[i, 3:4, :]
        size = member_ref[i, 4:5, :]
        phi = mass * (2.0 / size) - jnp.sum(total.T, axis=0, keepdims=True)
        phi_ref[i] = phi
        return energy + mass * phi

    energy = lax.fori_loop(0, slabs, step, jnp.zeros((1, TILE), F32), unroll=4 if slabs == group else 1)
    energy_ref[...] = 0.5 * jnp.sum(energy, axis=1, keepdims=True)


def final_kernel(mass_ref, dens_ref, back_ref, table_ref, energy_ref, count_ref, owner_ref, out_ref, pot_ref, total_ref, work_ref):
    total_ref[...] = energy_ref[...]
    out_ref[...] = (dens_ref[...] + back_ref[...]) * (DENSITY_SCALE / mass_ref[...])
    work_ref[...] = jnp.zeros_like(work_ref)
    lane = lax.broadcasted_iota(jnp.int32, (1, TILE), 1)

    def step(k, start):
        count = count_ref[0, k]
        block = start // TILE
        shift = start % TILE
        value = table_ref[owner_ref[0, k]]
        value = pltpu.roll(jnp.where(lane < count, value, 0.0), shift, 1)
        work_ref[pl.ds(block, 1), :] += jnp.where(lane >= shift, value, 0.0)
        work_ref[pl.ds(block + 1, 1), :] += jnp.where(lane < shift, value, 0.0)
        return start + count

    lax.fori_loop(0, count_ref.shape[1], step, jnp.int32(0), unroll=8)
    pot_ref[...] = work_ref[: pot_ref.shape[0], :]


def per_device(positions, masses, smoothing, block_lists, block_counts, group_owner):
    row_count = masses.shape[1]
    blocks = row_count // TILE
    slabs = lax.axis_size("slab")
    grps = lax.axis_size("grp")
    particles = (
        positions[0].reshape(3, blocks, TILE),
        masses.reshape(blocks, TILE),
        smoothing.reshape(blocks, TILE),
    )
    grid_shape = jax.ShapeDtypeStruct((blocks, TILE), F32)
    row_shape = jax.ShapeDtypeStruct((slabs, 1, TILE), F32)
    dma = pltpu.SemaphoreType.DMA
    density, table, back, energy = pl.pallas_call(
        functools.partial(main_kernel, slabs, grps),
        out_shape=(grid_shape, row_shape, grid_shape, jax.ShapeDtypeStruct((1, 1), F32)),
        in_specs=[VMEM, VMEM, VMEM, SMEM, SMEM, SMEM],
        out_specs=(VMEM, VMEM, VMEM, VMEM),
        scratch_shapes=[
            pltpu.VMEM((3, blocks, TILE), F32),
            pltpu.VMEM((blocks, TILE), F32),
            pltpu.VMEM((blocks, TILE), F32),
            pltpu.VMEM((slabs, 8, TILE), F32),
            pltpu.VMEM((slabs, 8, TILE), F32),
            pltpu.VMEM((slabs, 1, TILE), F32),
            pltpu.VMEM((KX * blocks, TILE), F32),
            pltpu.VMEM((blocks, TILE), F32),
            pltpu.VMEM((blocks, TILE, DEPTH), HALF),
            pltpu.VMEM((blocks, DEPTH, 3 * TILE), HALF),
            pltpu.VMEM((blocks, TILE, DEPTH), HALF),
            pltpu.VMEM((KO * TILE, 3 * TILE), F32),
            pltpu.VMEM((KO * TILE, 3 * TILE), F32),
            pltpu.VMEM((KX * TILE, 3 * TILE), F32),
            pltpu.VMEM((KX * TILE, 3 * TILE), F32),
            pltpu.VMEM((48, slabs * TILE), HALF),
            pltpu.VMEM((48, slabs * TILE), HALF),
            pltpu.VMEM((PLANES, blocks, TILE), F32),
            dma((slabs,)),
            dma((slabs,)),
            dma((slabs,)),
            dma((slabs,)),
            dma((3,)),
            dma((3,)),
            dma,
            dma,
        ],
        compiler_params=pltpu.CompilerParams(
            collective_id=0,
            has_side_effects=True,
        ),
    )(*particles, block_lists[0].T, block_counts, group_owner)
    density, potential, energy = pl.pallas_call(
        final_kernel,
        out_shape=(grid_shape, grid_shape, jax.ShapeDtypeStruct((1, 1), F32)),
        in_specs=[VMEM, VMEM, VMEM, VMEM, VMEM, SMEM, SMEM],
        out_specs=(VMEM, VMEM, VMEM),
        scratch_shapes=[pltpu.VMEM((blocks + 8, TILE), F32)],
    )(particles[1], density, back, table, energy, block_counts, group_owner)
    return (density.reshape(1, row_count), potential.reshape(1, row_count), energy)


def solution(mesh):
    placed = (
        P(("slab", "grp"), None, None),
        P(("slab", "grp"), None),
        P(("slab", "grp"), None),
        P(("slab", "grp"), None, None),
        P(("slab", "grp"), None),
        P("grp", None),
    )
    return jax.shard_map(
        per_device,
        mesh=mesh,
        in_specs=placed,
        out_specs=(P(("slab", "grp"), None), P(("slab", "grp"), None), P("grp", "slab")),
        check_vma=False,
    )
```

```python
import functools
import math

import jax
import jax.numpy as jnp
from jax import lax
from jax.experimental import pallas as pl
from jax.experimental.pallas import tpu as pltpu
from jax.sharding import PartitionSpec as P

TILE = 128
KX = 2
KO = 4
F32 = jnp.float32
HALF = jnp.bfloat16
DEPTH = 64
LOT = 8
OWN_LOTS = 4

DENSITY_SCALE = 21.0 / (256.0 * math.pi) / 16.0

VMEM = pl.BlockSpec(memory_space=pltpu.VMEM)
MESH = pl.DeviceIdType.MESH
SMEM = pl.BlockSpec(memory_space=pltpu.SMEM)


def split3(a):
    high = a.astype(HALF).astype(F32)
    rest = a - high
    mid = rest.astype(HALF).astype(F32)
    return high, mid, rest - mid


def left_six(a):
    high, mid, low = split3(a)
    return [high, high, mid, high, low, mid]


def right_six(a):
    high, mid, low = split3(a)
    return [high, mid, high, low, high, mid]


def left_rows(a):
    return jnp.concatenate(left_six(a), axis=0).astype(HALF)


def right_rows(a):
    return jnp.concatenate(right_six(a), axis=0).astype(HALF)


def centred(particles, lift):
    row = lax.broadcasted_iota(jnp.int32, particles.shape, 0)
    shift = jnp.where(row == 0, lift - 0.5, jnp.where(row < 3, -0.5, 0.0))
    coords = jnp.where(row < 3, particles + shift, 0.0)
    norm = jnp.sum(coords * coords, axis=0, keepdims=True)
    return row, coords, norm


FACTORS = 8
NORM, SIZE, PLANES = 8, 11, 14


def fill_planes(parts, plane_ref, lift):
    place_ref, mass_ref, size_ref = parts

    def step(i, _):
        rows = pl.ds(pl.multiple_of(i * LOT, LOT), LOT)
        coords = [place_ref[axis, rows, :] + ((lift if axis == 0 else 0.0) - 0.5) for axis in range(3)]
        norm = coords[0] * coords[0] + coords[1] * coords[1] + coords[2] * coords[2]
        size = size_ref[rows, :]
        planes = coords + [lax.rsqrt(mass_ref[rows, :])]
        for _ in range(4):
            planes.append(planes[-1] * size)
        planes += list(split3(norm)) + list(split3(size))
        for n, plane in enumerate(planes):
            plane_ref[n, rows, :] = plane
        return 0

    lax.fori_loop(0, mass_ref.shape[0] // LOT, step, 0, unroll=2)


def by_row(values):
    row = lax.broadcasted_iota(jnp.int32, (8, TILE), 0)
    block = jnp.broadcast_to(values[0], (8, TILE))
    for n, value in enumerate(values[1:]):
        block = jnp.where(row == n + 1, value, block)
    return block


def fill(parts, plane_ref, left_ref, right_ref, lift):
    fill_planes(parts, plane_ref, lift)
    row = lax.broadcasted_iota(jnp.int32, (8, TILE), 0)
    zero = jnp.zeros((8, TILE), F32)

    def step(i, _):
        plane = [plane_ref[n, pl.ds(i, 1), :] for n in range(PLANES)]
        coords, powers, norm, size = plane[:3], plane[3:8], plane[NORM:SIZE], plane[SIZE:]
        high, mid, low = split3(by_row(coords + powers[::-1]))
        rest = by_row(norm + [1.0, 1.0, 1.0] + size[:2])
        last = jnp.where(row == 0, size[2], 0.0)
        left_ref[i] = jnp.concatenate([high, high, high, mid, mid, low, rest, last], axis=0).astype(HALF).T
        if right_ref is not None:
            scale = by_row([-8.0, -8.0, -8.0, 0.0625, 0.25, 0.375, 0.25, 0.0625])
            parts3 = split3(scale * by_row(coords + powers))
            near = [jnp.where(row < 3, part, 0.0) for part in parts3]
            far = [jnp.where(row < 3, 0.0, part) for part in parts3]
            order = (0, 1, 2, 0, 1, 0)
            rest = by_row([4.0, 4.0, 4.0] + [4.0 * part for part in norm] + [0.0, 0.0])
            wide = by_row([0.0, 0.0, 0.0] + [2.0 * part for part in size] + [2.0, 2.0])
            last = jnp.where(row == 0, 2.0, 0.0)
            columns = (
                [near[n] for n in order] + [rest, zero],
                [zero] * 6 + [wide, last],
                [far[n] for n in order] + [zero, zero],
            )
            for m, column in enumerate(columns):
                right_ref[i, :, pl.ds(m * TILE, TILE)] = jnp.concatenate(column, axis=0).astype(HALF)
        return 0

    lax.fori_loop(0, left_ref.shape[0], step, 0, unroll=8)


def pair_dot(left, right, left_dim=0):
    return lax.dot_general(
        left, right, (((left_dim,), (0,)), ((), ())), preferred_element_type=F32
    )


def weights(both_ref, base):
    rows = pl.ds(base, 8)
    squared = jnp.maximum(both_ref[rows, :TILE], 1e-30)
    reach = both_ref[rows, TILE : 2 * TILE]
    near = jnp.maximum(reach - squared * lax.rsqrt(squared), 0.0)
    a = near * lax.rsqrt(both_ref[rows, 2 * TILE : 3 * TILE])
    a = a * a
    return (a * a) * (1.25 * reach - near)


def sweep(first, steps, end, fetch, use, even_ref, odd_ref, unroll):
    def step(i, _):
        b = first + 2 * i
        fetch(b + 1, odd_ref)
        use(b, even_ref)
        fetch(jnp.minimum(b + 2, end - 1), even_ref)
        use(b + 1, odd_ref)
        return 0

    lax.fori_loop(0, steps, step, 0, unroll=unroll)


def own_part(list_ref, dens_ref, left_ref, right_ref, even_ref, odd_ref):
    blocks = left_ref.shape[0]
    lot = blocks // OWN_LOTS

    def fetch(b, both_ref):
        right = right_ref[b]
        for k in range(KO):
            both_ref[pl.ds(k * TILE, TILE), :] = pair_dot(left_ref[list_ref[KX + k, b]], right, 1)

    def use(b, both_ref):
        total = jnp.zeros((8, TILE), F32)
        for base in range(0, KO * TILE, 8):
            total = total + weights(both_ref, base)
        dens_ref[pl.ds(b, 1), :] += jnp.sum(total, axis=0, keepdims=True)

    def lots(first, last):
        def one(i, _):
            sweep(i * lot, lot // 2, blocks, fetch, use, even_ref, odd_ref, lot // 2)
            return 0

        lax.fori_loop(first, last, one, 0)

    return functools.partial(fetch, 0, even_ref), lots


def cross_part(list_ref, dens_ref, column_ref, back_ref, far_ref, right_ref, even_ref, odd_ref):
    blocks = far_ref.shape[0]

    def fetch(b, both_ref):
        left = jnp.concatenate([far_ref[list_ref[k, b]] for k in range(KX)], axis=0)
        both_ref[...] = pair_dot(left, right_ref[b], 1)

    def use(b, both_ref):
        total = jnp.zeros((8, TILE), F32)
        for k in range(KX):
            values = [weights(both_ref, k * TILE + base) for base in range(0, TILE, 8)]
            for value in values:
                total = total + value
            column = jnp.concatenate(values, axis=0).T
            column_ref[pl.ds(KX * b + k, 1), :] = jnp.sum(column, axis=0, keepdims=True)
        dens_ref[pl.ds(b, 1), :] += jnp.sum(total, axis=0, keepdims=True)

    fetch(0, even_ref)
    sweep(0, blocks // 2, blocks, fetch, use, even_ref, odd_ref, math.gcd(blocks // 2, 8))

    lane = lax.broadcasted_iota(jnp.int32, (1, KX * blocks), 1)

    def name(b, row):
        for k in range(KX):
            row = jnp.where(lane == KX * b + k, list_ref[k, b], row)
        return row

    named = lax.fori_loop(0, blocks, name, jnp.zeros((1, KX * blocks), jnp.int32), unroll=8)
    block = lax.broadcasted_iota(jnp.int32, (blocks, KX * blocks), 0)
    chosen = jnp.where(block == named, 1.0, 0.0).astype(HALF)
    high, mid, low = split3(column_ref[...])
    back_ref[...] = sum(
        jnp.dot(chosen, part.astype(HALF), preferred_element_type=F32) for part in (low, mid, high)
    )


def main_kernel(
    slabs,
    grps,
    place_ref,
    weight_ref,
    size_ref,
    list_ref,
    count_ref,
    owner_ref,
    dens_ref,
    table_ref,
    back_ref,
    energy_ref,
    far_place_ref,
    far_weight_ref,
    far_size_ref,
    group_ref,
    member_ref,
    phi_ref,
    column_ref,
    sent_ref,
    left_ref,
    right_ref,
    far_ref,
    even_ref,
    odd_ref,
    near_even_ref,
    near_odd_ref,
    phi_target_ref,
    phi_source_ref,
    plane_ref,
    member_send,
    member_recv,
    phi_send,
    phi_recv,
    part_send,
    part_recv,
    back_send,
    back_recv,
):
    slab = lax.axis_index("slab")
    grp = lax.axis_index("grp")
    count = slabs * grps
    here = slab * grps + grp

    def place(index):
        return (index // grps, lax.rem(index, grps))

    above = place(lax.rem(here + 1, count))
    below = place(lax.rem(here + count - 1, count))

    def ahead(d):
        return lax.rem(slab + d, slabs)

    barrier = pltpu.get_barrier_semaphore()
    for other in (above, below):
        pl.semaphore_signal(barrier, inc=1, device_id=other, device_id_type=MESH)

    def greet(d, _):
        pl.semaphore_signal(barrier, inc=1, device_id=(ahead(d), grp), device_id_type=MESH)
        return 0

    lax.fori_loop(1, slabs, greet, 0)
    parts = (place_ref, weight_ref, size_ref)
    far_parts = (far_place_ref, far_weight_ref, far_size_ref)
    blocks = dens_ref.shape[0]
    ahead_lots = (here < 3 * count // 8).astype(jnp.int32) + (here < count // 32).astype(jnp.int32)
    prepare_own, own_lots = own_part(list_ref, dens_ref, left_ref, right_ref, even_ref, odd_ref)
    dens_ref[...] = jnp.zeros_like(dens_ref)
    fill(parts, plane_ref, left_ref, right_ref, 0.0)
    pick_groups(parts, count_ref, owner_ref, group_ref)
    prepare_own()
    own_lots(0, ahead_lots)
    pl.semaphore_wait(barrier, slabs + 1)

    def member_copy(d):
        return pltpu.make_async_remote_copy(
            src_ref=group_ref.at[ahead(d)],
            dst_ref=member_ref.at[slab],
            send_sem=member_send.at[d],
            recv_sem=member_recv.at[d],
            device_id=(ahead(d), grp),
            device_id_type=MESH,
        )

    def phi_copy(d):
        return pltpu.make_async_remote_copy(
            src_ref=phi_ref.at[ahead(d)],
            dst_ref=table_ref.at[slab],
            send_sem=phi_send.at[d],
            recv_sem=phi_recv.at[d],
            device_id=(ahead(d), grp),
            device_id_type=MESH,
        )

    part_copies = [
        pltpu.make_async_remote_copy(
            src_ref=near,
            dst_ref=far,
            send_sem=part_send.at[n],
            recv_sem=part_recv.at[n],
            device_id=above,
            device_id_type=MESH,
        )
        for n, (near, far) in enumerate(zip(parts, far_parts))
    ]
    back_copy = pltpu.make_async_remote_copy(
        src_ref=sent_ref,
        dst_ref=back_ref,
        send_sem=back_send,
        recv_sem=back_recv,
        device_id=below,
        device_id_type=MESH,
    )

    def each(action):
        def step(d, _):
            action(d)
            return 0

        lax.fori_loop(1, slabs, step, 0)

    each(lambda d: member_copy(d).start())
    for copy in part_copies:
        copy.start()

    own_lots(ahead_lots, OWN_LOTS - 1)

    member_ref[slab] = group_ref[slab]
    each(lambda d: member_copy(d).wait())
    phi_part(member_ref, phi_ref, energy_ref, phi_target_ref, phi_source_ref)
    each(lambda d: phi_copy(d).start())
    table_ref[slab] = phi_ref[slab]

    for copy in part_copies:
        copy.wait()
    fill(far_parts, plane_ref, far_ref, None, -1.0)
    cross_part(list_ref, dens_ref, column_ref, sent_ref, far_ref, right_ref, near_even_ref, near_odd_ref)
    back_copy.start()

    own_lots(OWN_LOTS - 1, OWN_LOTS)
    each(lambda d: phi_copy(d).wait())
    back_copy.wait()


def block_of(parts, i):
    place_ref, mass_ref, size_ref = parts
    row = lax.broadcasted_iota(jnp.int32, (8, TILE), 0)
    block = jnp.broadcast_to(size_ref[pl.ds(i, 1), :], (8, TILE))
    block = jnp.where(row == 3, mass_ref[pl.ds(i, 1), :], block)
    for axis in range(3):
        block = jnp.where(row == axis, place_ref[axis, pl.ds(i, 1), :], block)
    return block


def pick_groups(parts, count_ref, owner_ref, group_ref):
    blocks = parts[1].shape[0]
    row = lax.broadcasted_iota(jnp.int32, (8, TILE), 0)
    lane = lax.broadcasted_iota(jnp.int32, (8, TILE), 1)
    slot = lax.broadcasted_iota(jnp.int32, group_ref.shape, 0)

    def step(k, start):
        count = count_ref[0, k]
        block = jnp.minimum(start // TILE, blocks - 1)
        shift = start % TILE
        first = block_of(parts, block)
        second = block_of(parts, jnp.minimum(block + 1, blocks - 1))
        mixed = pltpu.roll(jnp.where(lane >= shift, first, second), (TILE - shift) % TILE, 1)
        mixed = jnp.where((row == 3) & (lane >= count), 0.0, mixed)
        group_ref[...] = jnp.where(slot == owner_ref[0, k], mixed, group_ref[...])
        return start + count

    group_ref[...] = jnp.zeros_like(group_ref)
    groups = count_ref.shape[1]
    lax.fori_loop(0, groups, step, jnp.int32(0), unroll=math.gcd(groups, 8))


def phi_part(member_ref, phi_ref, energy_ref, target_ref, source_ref):
    slabs = member_ref.shape[0]
    group = math.gcd(slabs, 8)

    def fill(i, _):
        particles = member_ref[i]
        row, coords, norm = centred(particles, 0.0)
        size = particles[4:5]
        norm = norm + 0.125 * size * size
        base = pl.multiple_of(i * TILE, TILE)
        source_ref[:, pl.ds(base, TILE)] = right_rows(
            jnp.where(row < 3, coords, jnp.where(row == 3, norm, jnp.where(row == 4, 1.0, 0.0)))
        )
        target_ref[:, pl.ds(base, TILE)] = left_rows(
            jnp.where(row < 3, -2.0 * coords, jnp.where(row == 3, 1.0, jnp.where(row == 4, norm, 0.0)))
        )
        return 0

    lax.fori_loop(0, slabs, fill, 0)

    def step(i, energy):
        target = target_ref[:, pl.ds(pl.multiple_of(i * TILE, TILE), TILE)]

        def inner(j, total):
            for n in range(group):
                base = pl.multiple_of((j * group + n) * TILE, TILE)
                pairs = pair_dot(target, source_ref[:, pl.ds(base, TILE)])
                total = total + lax.rsqrt(pairs) * member_ref[j * group + n, 3:4, :]
            return total

        total = lax.fori_loop(0, slabs // group, inner, jnp.zeros((TILE, TILE), F32), unroll=slabs == group)
        mass = member_ref[i, 3:4, :]
        size = member_ref[i, 4:5, :]
        phi = mass * (2.0 / size) - jnp.sum(total.T, axis=0, keepdims=True)
        phi_ref[i] = phi
        return energy + mass * phi

    energy = lax.fori_loop(0, slabs, step, jnp.zeros((1, TILE), F32), unroll=4 if slabs == group else 1)
    energy_ref[...] = 0.5 * jnp.sum(energy, axis=1, keepdims=True)


def final_kernel(mass_ref, dens_ref, back_ref, table_ref, energy_ref, count_ref, owner_ref, out_ref, pot_ref, total_ref, work_ref):
    total_ref[...] = energy_ref[...]
    out_ref[...] = (dens_ref[...] + back_ref[...]) * (DENSITY_SCALE / mass_ref[...])
    work_ref[...] = jnp.zeros_like(work_ref)
    lane = lax.broadcasted_iota(jnp.int32, (1, TILE), 1)

    def step(k, start):
        count = count_ref[0, k]
        block = start // TILE
        shift = start % TILE
        value = table_ref[owner_ref[0, k]]
        value = pltpu.roll(jnp.where(lane < count, value, 0.0), shift, 1)
        work_ref[pl.ds(block, 1), :] += jnp.where(lane >= shift, value, 0.0)
        work_ref[pl.ds(block + 1, 1), :] += jnp.where(lane < shift, value, 0.0)
        return start + count

    lax.fori_loop(0, count_ref.shape[1], step, jnp.int32(0), unroll=8)
    pot_ref[...] = work_ref[: pot_ref.shape[0], :]


def per_device(positions, masses, smoothing, block_lists, block_counts, group_owner):
    row_count = masses.shape[1]
    blocks = row_count // TILE
    slabs = lax.axis_size("slab")
    grps = lax.axis_size("grp")
    particles = (
        positions[0].reshape(3, blocks, TILE),
        masses.reshape(blocks, TILE),
        smoothing.reshape(blocks, TILE),
    )
    grid_shape = jax.ShapeDtypeStruct((blocks, TILE), F32)
    row_shape = jax.ShapeDtypeStruct((slabs, 1, TILE), F32)
    dma = pltpu.SemaphoreType.DMA
    density, table, back, energy = pl.pallas_call(
        functools.partial(main_kernel, slabs, grps),
        out_shape=(grid_shape, row_shape, grid_shape, jax.ShapeDtypeStruct((1, 1), F32)),
        in_specs=[VMEM, VMEM, VMEM, SMEM, SMEM, SMEM],
        out_specs=(VMEM, VMEM, VMEM, VMEM),
        scratch_shapes=[
            pltpu.VMEM((3, blocks, TILE), F32),
            pltpu.VMEM((blocks, TILE), F32),
            pltpu.VMEM((blocks, TILE), F32),
            pltpu.VMEM((slabs, 8, TILE), F32),
            pltpu.VMEM((slabs, 8, TILE), F32),
            pltpu.VMEM((slabs, 1, TILE), F32),
            pltpu.VMEM((KX * blocks, TILE), F32),
            pltpu.VMEM((blocks, TILE), F32),
            pltpu.VMEM((blocks, TILE, DEPTH), HALF),
            pltpu.VMEM((blocks, DEPTH, 3 * TILE), HALF),
            pltpu.VMEM((blocks, TILE, DEPTH), HALF),
            pltpu.VMEM((KO * TILE, 3 * TILE), F32),
            pltpu.VMEM((KO * TILE, 3 * TILE), F32),
            pltpu.VMEM((KX * TILE, 3 * TILE), F32),
            pltpu.VMEM((KX * TILE, 3 * TILE), F32),
            pltpu.VMEM((48, slabs * TILE), HALF),
            pltpu.VMEM((48, slabs * TILE), HALF),
            pltpu.VMEM((PLANES, blocks, TILE), F32),
            dma((slabs,)),
            dma((slabs,)),
            dma((slabs,)),
            dma((slabs,)),
            dma((3,)),
            dma((3,)),
            dma,
            dma,
        ],
        compiler_params=pltpu.CompilerParams(
            collective_id=0,
            has_side_effects=True,
        ),
    )(*particles, block_lists[0].T, block_counts, group_owner)
    density, potential, energy = pl.pallas_call(
        final_kernel,
        out_shape=(grid_shape, grid_shape, jax.ShapeDtypeStruct((1, 1), F32)),
        in_specs=[VMEM, VMEM, VMEM, VMEM, VMEM, SMEM, SMEM],
        out_specs=(VMEM, VMEM, VMEM),
        scratch_shapes=[pltpu.VMEM((blocks + 8, TILE), F32)],
    )(particles[1], density, back, table, energy, block_counts, group_owner)
    return (density.reshape(1, row_count), potential.reshape(1, row_count), energy)


def solution(mesh):
    placed = (
        P(("slab", "grp"), None, None),
        P(("slab", "grp"), None),
        P(("slab", "grp"), None),
        P(("slab", "grp"), None, None),
        P(("slab", "grp"), None),
        P("grp", None),
    )
    return jax.shard_map(
        per_device,
        mesh=mesh,
        in_specs=placed,
        out_specs=(P(("slab", "grp"), None), P(("slab", "grp"), None), P("grp", "slab")),
        check_vma=False,
    )
```

```python
import functools
import math

import jax
import jax.numpy as jnp
from jax import lax
from jax.experimental import pallas as pl
from jax.experimental.pallas import tpu as pltpu
from jax.sharding import PartitionSpec as P

TILE = 128
KX = 2
KO = 4
F32 = jnp.float32
HALF = jnp.bfloat16
DEPTH = 64
LOT = 8
OWN_LOTS = 8
MID_LOTS = 5

DENSITY_SCALE = 21.0 / (256.0 * math.pi) / 16.0

VMEM = pl.BlockSpec(memory_space=pltpu.VMEM)
MESH = pl.DeviceIdType.MESH
SMEM = pl.BlockSpec(memory_space=pltpu.SMEM)


def split3(a):
    high = a.astype(HALF).astype(F32)
    rest = a - high
    mid = rest.astype(HALF).astype(F32)
    return high, mid, rest - mid


def left_six(a):
    high, mid, low = split3(a)
    return [high, high, mid, high, low, mid]


def right_six(a):
    high, mid, low = split3(a)
    return [high, mid, high, low, high, mid]


def left_rows(a):
    return jnp.concatenate(left_six(a), axis=0).astype(HALF)


def right_rows(a):
    return jnp.concatenate(right_six(a), axis=0).astype(HALF)


def centred(particles, lift):
    row = lax.broadcasted_iota(jnp.int32, particles.shape, 0)
    shift = jnp.where(row == 0, lift - 0.5, jnp.where(row < 3, -0.5, 0.0))
    coords = jnp.where(row < 3, particles + shift, 0.0)
    norm = jnp.sum(coords * coords, axis=0, keepdims=True)
    return row, coords, norm


FACTORS = 8
NORM, SIZE, PLANES = 8, 11, 14


def fill_planes(parts, plane_ref, lift):
    place_ref, mass_ref, size_ref = parts

    def step(i, _):
        rows = pl.ds(pl.multiple_of(i * LOT, LOT), LOT)
        coords = [place_ref[axis, rows, :] + ((lift if axis == 0 else 0.0) - 0.5) for axis in range(3)]
        norm = coords[0] * coords[0] + coords[1] * coords[1] + coords[2] * coords[2]
        size = size_ref[rows, :]
        planes = coords + [lax.rsqrt(mass_ref[rows, :])]
        for _ in range(4):
            planes.append(planes[-1] * size)
        planes += list(split3(norm)) + list(split3(size))
        for n, plane in enumerate(planes):
            plane_ref[n, rows, :] = plane
        return 0

    lax.fori_loop(0, mass_ref.shape[0] // LOT, step, 0, unroll=2)


def by_row(values):
    row = lax.broadcasted_iota(jnp.int32, (8, TILE), 0)
    block = jnp.broadcast_to(values[0], (8, TILE))
    for n, value in enumerate(values[1:]):
        block = jnp.where(row == n + 1, value, block)
    return block


def fill(parts, plane_ref, left_ref, right_ref, lift):
    fill_planes(parts, plane_ref, lift)
    row = lax.broadcasted_iota(jnp.int32, (8, TILE), 0)
    zero = jnp.zeros((8, TILE), F32)

    def step(i, _):
        plane = [plane_ref[n, pl.ds(i, 1), :] for n in range(PLANES)]
        coords, powers, norm, size = plane[:3], plane[3:8], plane[NORM:SIZE], plane[SIZE:]
        high, mid, low = split3(by_row(coords + powers[::-1]))
        rest = by_row(norm + [1.0, 1.0, 1.0] + size[:2])
        last = jnp.where(row == 0, size[2], 0.0)
        left_ref[i] = jnp.concatenate([high, high, high, mid, mid, low, rest, last], axis=0).astype(HALF).T
        if right_ref is not None:
            scale = by_row([-8.0, -8.0, -8.0, 0.0625, 0.25, 0.375, 0.25, 0.0625])
            parts3 = split3(scale * by_row(coords + powers))
            near = [jnp.where(row < 3, part, 0.0) for part in parts3]
            far = [jnp.where(row < 3, 0.0, part) for part in parts3]
            order = (0, 1, 2, 0, 1, 0)
            rest = by_row([4.0, 4.0, 4.0] + [4.0 * part for part in norm] + [0.0, 0.0])
            wide = by_row([0.0, 0.0, 0.0] + [2.0 * part for part in size] + [2.0, 2.0])
            last = jnp.where(row == 0, 2.0, 0.0)
            columns = (
                [near[n] for n in order] + [rest, zero],
                [zero] * 6 + [wide, last],
                [far[n] for n in order] + [zero, zero],
            )
            for m, column in enumerate(columns):
                right_ref[i, :, pl.ds(m * TILE, TILE)] = jnp.concatenate(column, axis=0).astype(HALF)
        return 0

    lax.fori_loop(0, left_ref.shape[0], step, 0, unroll=8)


def pair_dot(left, right, left_dim=0):
    return lax.dot_general(
        left, right, (((left_dim,), (0,)), ((), ())), preferred_element_type=F32
    )


def weights(both_ref, base):
    rows = pl.ds(base, 8)
    squared = jnp.maximum(both_ref[rows, :TILE], 1e-30)
    reach = both_ref[rows, TILE : 2 * TILE]
    near = jnp.maximum(reach - squared * lax.rsqrt(squared), 0.0)
    a = near * lax.rsqrt(both_ref[rows, 2 * TILE : 3 * TILE])
    a = a * a
    return (a * a) * (1.25 * reach - near)


def sweep(first, steps, end, fetch, use, even_ref, odd_ref, unroll):
    def step(i, _):
        b = first + 2 * i
        fetch(b + 1, odd_ref)
        use(b, even_ref)
        fetch(jnp.minimum(b + 2, end - 1), even_ref)
        use(b + 1, odd_ref)
        return 0

    lax.fori_loop(0, steps, step, 0, unroll=unroll)


def own_part(list_ref, dens_ref, left_ref, right_ref, even_ref, odd_ref):
    blocks = left_ref.shape[0]
    lot = blocks // OWN_LOTS

    def fetch(b, both_ref):
        right = right_ref[b]
        for k in range(KO):
            both_ref[pl.ds(k * TILE, TILE), :] = pair_dot(left_ref[list_ref[KX + k, b]], right, 1)

    def use(b, both_ref):
        total = jnp.zeros((8, TILE), F32)
        for base in range(0, KO * TILE, 8):
            total = total + weights(both_ref, base)
        dens_ref[pl.ds(b, 1), :] += jnp.sum(total, axis=0, keepdims=True)

    def run(first, lots):
        steps = lots * lot // 2
        sweep(first * lot, steps, blocks, fetch, use, even_ref, odd_ref, steps)

    def loop(first, last):
        def one(i, _):
            run(i, 1)
            return 0

        lax.fori_loop(first, last, one, 0)

    return functools.partial(fetch, 0, even_ref), loop, run


def cross_part(list_ref, dens_ref, column_ref, back_ref, far_ref, right_ref, even_ref, odd_ref):
    blocks = far_ref.shape[0]

    def fetch(b, both_ref):
        left = jnp.concatenate([far_ref[list_ref[k, b]] for k in range(KX)], axis=0)
        both_ref[...] = pair_dot(left, right_ref[b], 1)

    def use(b, both_ref):
        total = jnp.zeros((8, TILE), F32)
        for k in range(KX):
            values = [weights(both_ref, k * TILE + base) for base in range(0, TILE, 8)]
            for value in values:
                total = total + value
            column = jnp.concatenate(values, axis=0).T
            column_ref[pl.ds(KX * b + k, 1), :] = jnp.sum(column, axis=0, keepdims=True)
        dens_ref[pl.ds(b, 1), :] += jnp.sum(total, axis=0, keepdims=True)

    fetch(0, even_ref)
    sweep(0, blocks // 2, blocks, fetch, use, even_ref, odd_ref, math.gcd(blocks // 2, 16))

    lane = lax.broadcasted_iota(jnp.int32, (1, KX * blocks), 1)

    def name(b, row):
        for k in range(KX):
            row = jnp.where(lane == KX * b + k, list_ref[k, b], row)
        return row

    named = lax.fori_loop(0, blocks, name, jnp.zeros((1, KX * blocks), jnp.int32), unroll=8)
    block = lax.broadcasted_iota(jnp.int32, (blocks, KX * blocks), 0)
    chosen = jnp.where(block == named, 1.0, 0.0).astype(HALF)
    high, mid, low = split3(column_ref[...])
    back_ref[...] = sum(
        jnp.dot(chosen, part.astype(HALF), preferred_element_type=F32) for part in (low, mid, high)
    )


def main_kernel(
    slabs,
    grps,
    place_ref,
    weight_ref,
    size_ref,
    list_ref,
    count_ref,
    owner_ref,
    dens_ref,
    table_ref,
    back_ref,
    energy_ref,
    far_place_ref,
    far_weight_ref,
    far_size_ref,
    group_ref,
    member_ref,
    phi_ref,
    column_ref,
    sent_ref,
    left_ref,
    right_ref,
    far_ref,
    even_ref,
    odd_ref,
    near_even_ref,
    near_odd_ref,
    phi_target_ref,
    phi_source_ref,
    plane_ref,
    member_send,
    member_recv,
    phi_send,
    phi_recv,
    part_send,
    part_recv,
    back_send,
    back_recv,
):
    slab = lax.axis_index("slab")
    grp = lax.axis_index("grp")
    count = slabs * grps
    here = slab * grps + grp

    def place(index):
        return (index // grps, lax.rem(index, grps))

    above = place(lax.rem(here + 1, count))
    below = place(lax.rem(here + count - 1, count))

    def ahead(d):
        return lax.rem(slab + d, slabs)

    barrier = pltpu.get_barrier_semaphore()
    for other in (above, below):
        pl.semaphore_signal(barrier, inc=1, device_id=other, device_id_type=MESH)

    def greet(d, _):
        pl.semaphore_signal(barrier, inc=1, device_id=(ahead(d), grp), device_id_type=MESH)
        return 0

    lax.fori_loop(1, slabs, greet, 0)
    parts = (place_ref, weight_ref, size_ref)
    far_parts = (far_place_ref, far_weight_ref, far_size_ref)
    blocks = dens_ref.shape[0]
    first_device = here < count // 32
    ahead_lots = sum((here < count * n // 32).astype(jnp.int32) for n in (1, 4, 12))
    extra = OWN_LOTS - 1 - MID_LOTS
    mid_lots = MID_LOTS + extra * first_device.astype(jnp.int32)
    prepare_own, own_loop, own_run = own_part(list_ref, dens_ref, left_ref, right_ref, even_ref, odd_ref)
    dens_ref[...] = jnp.zeros_like(dens_ref)
    fill(parts, plane_ref, left_ref, right_ref, 0.0)
    pick_groups(parts, count_ref, owner_ref, group_ref)
    prepare_own()
    own_loop(0, ahead_lots)
    pl.semaphore_wait(barrier, slabs + 1)

    def member_copy(d):
        return pltpu.make_async_remote_copy(
            src_ref=group_ref.at[ahead(d)],
            dst_ref=member_ref.at[slab],
            send_sem=member_send.at[d],
            recv_sem=member_recv.at[d],
            device_id=(ahead(d), grp),
            device_id_type=MESH,
        )

    def phi_copy(d):
        return pltpu.make_async_remote_copy(
            src_ref=phi_ref.at[ahead(d)],
            dst_ref=table_ref.at[slab],
            send_sem=phi_send.at[d],
            recv_sem=phi_recv.at[d],
            device_id=(ahead(d), grp),
            device_id_type=MESH,
        )

    part_copies = [
        pltpu.make_async_remote_copy(
            src_ref=near,
            dst_ref=far,
            send_sem=part_send.at[n],
            recv_sem=part_recv.at[n],
            device_id=above,
            device_id_type=MESH,
        )
        for n, (near, far) in enumerate(zip(parts, far_parts))
    ]
    back_copy = pltpu.make_async_remote_copy(
        src_ref=sent_ref,
        dst_ref=back_ref,
        send_sem=back_send,
        recv_sem=back_recv,
        device_id=below,
        device_id_type=MESH,
    )

    def each(action):
        def step(d, _):
            action(d)
            return 0

        lax.fori_loop(1, slabs, step, 0)

    each(lambda d: member_copy(d).start())
    for copy in part_copies:
        copy.start()

    own_loop(ahead_lots, mid_lots)

    member_ref[slab] = group_ref[slab]
    each(lambda d: member_copy(d).wait())
    phi_part(member_ref, phi_ref, energy_ref, phi_target_ref, phi_source_ref)
    each(lambda d: phi_copy(d).start())
    table_ref[slab] = phi_ref[slab]

    for copy in part_copies:
        copy.wait()
    fill(far_parts, plane_ref, far_ref, None, -1.0)
    cross_part(list_ref, dens_ref, column_ref, sent_ref, far_ref, right_ref, near_even_ref, near_odd_ref)
    back_copy.start()

    @pl.when(first_device)
    def _():
        own_run(MID_LOTS + extra, OWN_LOTS - MID_LOTS - extra)

    @pl.when(jnp.logical_not(first_device))
    def _():
        own_run(MID_LOTS, OWN_LOTS - MID_LOTS)

    each(lambda d: phi_copy(d).wait())
    back_copy.wait()


def block_of(parts, i):
    place_ref, mass_ref, size_ref = parts
    row = lax.broadcasted_iota(jnp.int32, (8, TILE), 0)
    block = jnp.broadcast_to(size_ref[pl.ds(i, 1), :], (8, TILE))
    block = jnp.where(row == 3, mass_ref[pl.ds(i, 1), :], block)
    for axis in range(3):
        block = jnp.where(row == axis, place_ref[axis, pl.ds(i, 1), :], block)
    return block


def pick_groups(parts, count_ref, owner_ref, group_ref):
    blocks = parts[1].shape[0]
    row = lax.broadcasted_iota(jnp.int32, (8, TILE), 0)
    lane = lax.broadcasted_iota(jnp.int32, (8, TILE), 1)
    slot = lax.broadcasted_iota(jnp.int32, group_ref.shape, 0)

    def step(k, start):
        count = count_ref[0, k]
        block = jnp.minimum(start // TILE, blocks - 1)
        shift = start % TILE
        first = block_of(parts, block)
        second = block_of(parts, jnp.minimum(block + 1, blocks - 1))
        mixed = pltpu.roll(jnp.where(lane >= shift, first, second), (TILE - shift) % TILE, 1)
        mixed = jnp.where((row == 3) & (lane >= count), 0.0, mixed)
        group_ref[...] = jnp.where(slot == owner_ref[0, k], mixed, group_ref[...])
        return start + count

    group_ref[...] = jnp.zeros_like(group_ref)
    groups = count_ref.shape[1]
    lax.fori_loop(0, groups, step, jnp.int32(0), unroll=math.gcd(groups, 8))


def phi_part(member_ref, phi_ref, energy_ref, target_ref, source_ref):
    slabs = member_ref.shape[0]
    group = math.gcd(slabs, 8)

    def fill(i, _):
        particles = member_ref[i]
        row, coords, norm = centred(particles, 0.0)
        size = particles[4:5]
        norm = norm + 0.125 * size * size
        base = pl.multiple_of(i * TILE, TILE)
        source_ref[:, pl.ds(base, TILE)] = right_rows(
            jnp.where(row < 3, coords, jnp.where(row == 3, norm, jnp.where(row == 4, 1.0, 0.0)))
        )
        target_ref[i] = left_rows(
            jnp.where(row < 3, -2.0 * coords, jnp.where(row == 3, 1.0, jnp.where(row == 4, norm, 0.0)))
        ).T
        return 0

    lax.fori_loop(0, slabs, fill, 0, unroll=group)

    def step(i, energy):
        target = target_ref[i]

        def inner(j, total):
            for n in range(group):
                base = pl.multiple_of((j * group + n) * TILE, TILE)
                pairs = pair_dot(target, source_ref[:, pl.ds(base, TILE)], 1)
                total = total + lax.rsqrt(pairs) * member_ref[j * group + n, 3:4, :]
            return total

        total = lax.fori_loop(0, slabs // group, inner, jnp.zeros((TILE, TILE), F32), unroll=slabs == group)
        mass = member_ref[i, 3:4, :]
        size = member_ref[i, 4:5, :]
        phi = mass * (2.0 / size) - jnp.sum(total.T, axis=0, keepdims=True)
        phi_ref[i] = phi
        return energy + mass * phi

    energy = lax.fori_loop(0, slabs, step, jnp.zeros((1, TILE), F32), unroll=8 if slabs == group else 1)
    energy_ref[...] = 0.5 * jnp.sum(energy, axis=1, keepdims=True)


def final_kernel(mass_ref, dens_ref, back_ref, table_ref, energy_ref, count_ref, owner_ref, out_ref, pot_ref, total_ref, work_ref):
    total_ref[...] = energy_ref[...]
    out_ref[...] = (dens_ref[...] + back_ref[...]) * (DENSITY_SCALE / mass_ref[...])
    work_ref[...] = jnp.zeros_like(work_ref)
    lane = lax.broadcasted_iota(jnp.int32, (1, TILE), 1)

    def step(k, start):
        count = count_ref[0, k]
        block = start // TILE
        shift = start % TILE
        value = table_ref[owner_ref[0, k]]
        value = pltpu.roll(jnp.where(lane < count, value, 0.0), shift, 1)
        work_ref[pl.ds(block, 1), :] += jnp.where(lane >= shift, value, 0.0)
        work_ref[pl.ds(block + 1, 1), :] += jnp.where(lane < shift, value, 0.0)
        return start + count

    lax.fori_loop(0, count_ref.shape[1], step, jnp.int32(0), unroll=8)
    pot_ref[...] = work_ref[: pot_ref.shape[0], :]


def per_device(positions, masses, smoothing, block_lists, block_counts, group_owner):
    row_count = masses.shape[1]
    blocks = row_count // TILE
    slabs = lax.axis_size("slab")
    grps = lax.axis_size("grp")
    particles = (
        positions[0].reshape(3, blocks, TILE),
        masses.reshape(blocks, TILE),
        smoothing.reshape(blocks, TILE),
    )
    grid_shape = jax.ShapeDtypeStruct((blocks, TILE), F32)
    row_shape = jax.ShapeDtypeStruct((slabs, 1, TILE), F32)
    dma = pltpu.SemaphoreType.DMA
    density, table, back, energy = pl.pallas_call(
        functools.partial(main_kernel, slabs, grps),
        out_shape=(grid_shape, row_shape, grid_shape, jax.ShapeDtypeStruct((1, 1), F32)),
        in_specs=[VMEM, VMEM, VMEM, SMEM, SMEM, SMEM],
        out_specs=(VMEM, VMEM, VMEM, VMEM),
        scratch_shapes=[
            pltpu.VMEM((3, blocks, TILE), F32),
            pltpu.VMEM((blocks, TILE), F32),
            pltpu.VMEM((blocks, TILE), F32),
            pltpu.VMEM((slabs, 8, TILE), F32),
            pltpu.VMEM((slabs, 8, TILE), F32),
            pltpu.VMEM((slabs, 1, TILE), F32),
            pltpu.VMEM((KX * blocks, TILE), F32),
            pltpu.VMEM((blocks, TILE), F32),
            pltpu.VMEM((blocks, TILE, DEPTH), HALF),
            pltpu.VMEM((blocks, DEPTH, 3 * TILE), HALF),
            pltpu.VMEM((blocks, TILE, DEPTH), HALF),
            pltpu.VMEM((KO * TILE, 3 * TILE), F32),
            pltpu.VMEM((KO * TILE, 3 * TILE), F32),
            pltpu.VMEM((KX * TILE, 3 * TILE), F32),
            pltpu.VMEM((KX * TILE, 3 * TILE), F32),
            pltpu.VMEM((slabs, TILE, 48), HALF),
            pltpu.VMEM((48, slabs * TILE), HALF),
            pltpu.VMEM((PLANES, blocks, TILE), F32),
            dma((slabs,)),
            dma((slabs,)),
            dma((slabs,)),
            dma((slabs,)),
            dma((3,)),
            dma((3,)),
            dma,
            dma,
        ],
        compiler_params=pltpu.CompilerParams(
            collective_id=0,
            has_side_effects=True,
        ),
    )(*particles, block_lists[0].T, block_counts, group_owner)
    density, potential, energy = pl.pallas_call(
        final_kernel,
        out_shape=(grid_shape, grid_shape, jax.ShapeDtypeStruct((1, 1), F32)),
        in_specs=[VMEM, VMEM, VMEM, VMEM, VMEM, SMEM, SMEM],
        out_specs=(VMEM, VMEM, VMEM),
        scratch_shapes=[pltpu.VMEM((blocks + 8, TILE), F32)],
    )(particles[1], density, back, table, energy, block_counts, group_owner)
    return (density.reshape(1, row_count), potential.reshape(1, row_count), energy)


def solution(mesh):
    placed = (
        P(("slab", "grp"), None, None),
        P(("slab", "grp"), None),
        P(("slab", "grp"), None),
        P(("slab", "grp"), None, None),
        P(("slab", "grp"), None),
        P("grp", None),
    )
    return jax.shard_map(
        per_device,
        mesh=mesh,
        in_specs=placed,
        out_specs=(P(("slab", "grp"), None), P(("slab", "grp"), None), P("grp", "slab")),
        check_vma=False,
    )
```

```python
import functools
import math

import jax
import jax.numpy as jnp
from jax import lax
from jax.experimental import pallas as pl
from jax.experimental.pallas import tpu as pltpu
from jax.sharding import PartitionSpec as P

TILE = 128
KX = 2
KO = 4
F32 = jnp.float32
HALF = jnp.bfloat16
DEPTH = 64
LOT = 8
OWN_LOTS = 8
MID_LOTS = 5

DENSITY_SCALE = 21.0 / (256.0 * math.pi) / 16.0

VMEM = pl.BlockSpec(memory_space=pltpu.VMEM)
MESH = pl.DeviceIdType.MESH
SMEM = pl.BlockSpec(memory_space=pltpu.SMEM)


def split3(a):
    high = a.astype(HALF).astype(F32)
    rest = a - high
    mid = rest.astype(HALF).astype(F32)
    return high, mid, rest - mid


def left_six(a):
    high, mid, low = split3(a)
    return [high, high, mid, high, low, mid]


def right_six(a):
    high, mid, low = split3(a)
    return [high, mid, high, low, high, mid]


def left_rows(a):
    return jnp.concatenate(left_six(a), axis=0).astype(HALF)


def right_rows(a):
    return jnp.concatenate(right_six(a), axis=0).astype(HALF)


def centred(particles, lift):
    row = lax.broadcasted_iota(jnp.int32, particles.shape, 0)
    shift = jnp.where(row == 0, lift - 0.5, jnp.where(row < 3, -0.5, 0.0))
    coords = jnp.where(row < 3, particles + shift, 0.0)
    norm = jnp.sum(coords * coords, axis=0, keepdims=True)
    return row, coords, norm


FACTORS = 8
NORM, SIZE, PLANES = 8, 11, 14


def fill_planes(parts, plane_ref, lift):
    place_ref, mass_ref, size_ref = parts

    def step(i, _):
        rows = pl.ds(pl.multiple_of(i * LOT, LOT), LOT)
        coords = [place_ref[axis, rows, :] + ((lift if axis == 0 else 0.0) - 0.5) for axis in range(3)]
        norm = coords[0] * coords[0] + coords[1] * coords[1] + coords[2] * coords[2]
        size = size_ref[rows, :]
        planes = coords + [lax.rsqrt(mass_ref[rows, :])]
        for _ in range(4):
            planes.append(planes[-1] * size)
        planes += list(split3(norm)) + list(split3(size))
        for n, plane in enumerate(planes):
            plane_ref[n, rows, :] = plane
        return 0

    lax.fori_loop(0, mass_ref.shape[0] // LOT, step, 0, unroll=2)


def by_row(values):
    row = lax.broadcasted_iota(jnp.int32, (8, TILE), 0)
    block = jnp.broadcast_to(values[0], (8, TILE))
    for n, value in enumerate(values[1:]):
        block = jnp.where(row == n + 1, value, block)
    return block


def fill(parts, plane_ref, left_ref, right_ref, lift):
    fill_planes(parts, plane_ref, lift)
    row = lax.broadcasted_iota(jnp.int32, (8, TILE), 0)
    zero = jnp.zeros((8, TILE), F32)

    def step(i, _):
        plane = [plane_ref[n, pl.ds(i, 1), :] for n in range(PLANES)]
        coords, powers, norm, size = plane[:3], plane[3:8], plane[NORM:SIZE], plane[SIZE:]
        high, mid, low = split3(by_row(coords + powers[::-1]))
        rest = by_row(norm + [1.0, 1.0, 1.0] + size[:2])
        last = jnp.where(row == 0, size[2], 0.0)
        left_ref[i] = jnp.concatenate([high, high, high, mid, mid, low, rest, last], axis=0).astype(HALF).T
        if right_ref is not None:
            scale = by_row([-8.0, -8.0, -8.0, 0.0625, 0.25, 0.375, 0.25, 0.0625])
            parts3 = split3(scale * by_row(coords + powers))
            near = [jnp.where(row < 3, part, 0.0) for part in parts3]
            far = [jnp.where(row < 3, 0.0, part) for part in parts3]
            order = (0, 1, 2, 0, 1, 0)
            rest = by_row([4.0, 4.0, 4.0] + [4.0 * part for part in norm] + [0.0, 0.0])
            wide = by_row([0.0, 0.0, 0.0] + [2.0 * part for part in size] + [2.0, 2.0])
            last = jnp.where(row == 0, 2.0, 0.0)
            columns = (
                [near[n] for n in order] + [rest, zero],
                [zero] * 6 + [wide, last],
                [far[n] for n in order] + [zero, zero],
            )
            for m, column in enumerate(columns):
                right_ref[i, :, pl.ds(m * TILE, TILE)] = jnp.concatenate(column, axis=0).astype(HALF)
        return 0

    lax.fori_loop(0, left_ref.shape[0], step, 0, unroll=8)


def pair_dot(left, right, left_dim=0):
    return lax.dot_general(
        left, right, (((left_dim,), (0,)), ((), ())), preferred_element_type=F32
    )


def weights(both_ref, base):
    rows = pl.ds(base, 8)
    squared = jnp.maximum(both_ref[rows, :TILE], 1e-30)
    reach = both_ref[rows, TILE : 2 * TILE]
    near = jnp.maximum(reach - squared * lax.rsqrt(squared), 0.0)
    a = near * lax.rsqrt(both_ref[rows, 2 * TILE : 3 * TILE])
    a = a * a
    return (a * a) * (1.25 * reach - near)


def sweep(first, steps, end, fetch, use, even_ref, odd_ref, unroll):
    def step(i, _):
        b = first + 2 * i
        fetch(b + 1, odd_ref)
        use(b, even_ref)
        fetch(jnp.minimum(b + 2, end - 1), even_ref)
        use(b + 1, odd_ref)
        return 0

    lax.fori_loop(0, steps, step, 0, unroll=unroll)


def own_part(list_ref, dens_ref, left_ref, right_ref, even_ref, odd_ref):
    blocks = left_ref.shape[0]
    lot = blocks // OWN_LOTS

    def fetch(b, both_ref):
        right = right_ref[b]
        for k in range(KO):
            both_ref[pl.ds(k * TILE, TILE), :] = pair_dot(left_ref[list_ref[KX + k, b]], right, 1)

    def use(b, both_ref):
        total = jnp.zeros((8, TILE), F32)
        for base in range(0, KO * TILE, 8):
            total = total + weights(both_ref, base)
        dens_ref[pl.ds(b, 1), :] += jnp.sum(total, axis=0, keepdims=True)

    def run(first, lots):
        steps = lots * lot // 2
        sweep(first * lot, steps, blocks, fetch, use, even_ref, odd_ref, steps)

    def loop(first, last):
        def one(i, _):
            run(i, 1)
            return 0

        lax.fori_loop(first, last, one, 0)

    return functools.partial(fetch, 0, even_ref), loop, run


def cross_part(list_ref, dens_ref, column_ref, back_ref, far_ref, right_ref, even_ref, odd_ref):
    blocks = far_ref.shape[0]

    def fetch(b, both_ref):
        left = jnp.concatenate([far_ref[list_ref[k, b]] for k in range(KX)], axis=0)
        both_ref[...] = pair_dot(left, right_ref[b], 1)

    def use(b, both_ref):
        total = jnp.zeros((8, TILE), F32)
        for k in range(KX):
            values = [weights(both_ref, k * TILE + base) for base in range(0, TILE, 8)]
            for value in values:
                total = total + value
            column = jnp.concatenate(values, axis=0).T
            column_ref[pl.ds(KX * b + k, 1), :] = jnp.sum(column, axis=0, keepdims=True)
        dens_ref[pl.ds(b, 1), :] += jnp.sum(total, axis=0, keepdims=True)

    fetch(0, even_ref)
    sweep(0, blocks // 2, blocks, fetch, use, even_ref, odd_ref, math.gcd(blocks // 2, 16))

    lane = lax.broadcasted_iota(jnp.int32, (1, KX * blocks), 1)

    def name(b, row):
        for k in range(KX):
            row = jnp.where(lane == KX * b + k, list_ref[k, b], row)
        return row

    named = lax.fori_loop(0, blocks, name, jnp.zeros((1, KX * blocks), jnp.int32), unroll=8)
    block = lax.broadcasted_iota(jnp.int32, (blocks, KX * blocks), 0)
    chosen = jnp.where(block == named, 1.0, 0.0).astype(HALF)
    high, mid, low = split3(column_ref[...])
    back_ref[...] = sum(
        jnp.dot(chosen, part.astype(HALF), preferred_element_type=F32) for part in (low, mid, high)
    )


def main_kernel(
    slabs,
    grps,
    place_ref,
    weight_ref,
    size_ref,
    list_ref,
    count_ref,
    owner_ref,
    dens_ref,
    rest_ref,
    table_ref,
    back_ref,
    energy_ref,
    far_place_ref,
    far_weight_ref,
    far_size_ref,
    group_ref,
    member_ref,
    phi_ref,
    column_ref,
    sent_ref,
    left_ref,
    right_ref,
    far_ref,
    even_ref,
    odd_ref,
    near_even_ref,
    near_odd_ref,
    phi_target_ref,
    phi_source_ref,
    plane_ref,
    member_send,
    member_recv,
    phi_send,
    phi_recv,
    part_send,
    part_recv,
    back_send,
    back_recv,
):
    slab = lax.axis_index("slab")
    grp = lax.axis_index("grp")
    count = slabs * grps
    here = slab * grps + grp

    def place(index):
        return (index // grps, lax.rem(index, grps))

    above = place(lax.rem(here + 1, count))
    below = place(lax.rem(here + count - 1, count))

    def ahead(d):
        return lax.rem(slab + d, slabs)

    barrier = pltpu.get_barrier_semaphore()
    for other in (above, below):
        pl.semaphore_signal(barrier, inc=1, device_id=other, device_id_type=MESH)

    def greet(d, _):
        pl.semaphore_signal(barrier, inc=1, device_id=(ahead(d), grp), device_id_type=MESH)
        return 0

    lax.fori_loop(1, slabs, greet, 0)
    parts = (place_ref, weight_ref, size_ref)
    far_parts = (far_place_ref, far_weight_ref, far_size_ref)
    blocks = dens_ref.shape[0]
    first_device = here < count // 32
    ahead_lots = sum((here < count * n // 32).astype(jnp.int32) for n in (1, 4, 12))
    extra = OWN_LOTS - 1 - MID_LOTS
    mid_lots = MID_LOTS + extra * first_device.astype(jnp.int32)
    prepare_own, own_loop, own_run = own_part(list_ref, dens_ref, left_ref, right_ref, even_ref, odd_ref)
    dens_ref[...] = jnp.zeros_like(dens_ref)
    fill(parts, plane_ref, left_ref, right_ref, 0.0)
    pick_groups(parts, count_ref, owner_ref, group_ref)
    prepare_own()
    own_loop(0, ahead_lots)
    pl.semaphore_wait(barrier, slabs + 1)

    def member_copy(d):
        return pltpu.make_async_remote_copy(
            src_ref=group_ref.at[ahead(d)],
            dst_ref=member_ref.at[slab],
            send_sem=member_send.at[d],
            recv_sem=member_recv.at[d],
            device_id=(ahead(d), grp),
            device_id_type=MESH,
        )

    def phi_copy(d):
        return pltpu.make_async_remote_copy(
            src_ref=phi_ref.at[ahead(d)],
            dst_ref=table_ref.at[slab],
            send_sem=phi_send.at[d],
            recv_sem=phi_recv.at[d],
            device_id=(ahead(d), grp),
            device_id_type=MESH,
        )

    part_copies = [
        pltpu.make_async_remote_copy(
            src_ref=near,
            dst_ref=far,
            send_sem=part_send.at[n],
            recv_sem=part_recv.at[n],
            device_id=above,
            device_id_type=MESH,
        )
        for n, (near, far) in enumerate(zip(parts, far_parts))
    ]
    back_copy = pltpu.make_async_remote_copy(
        src_ref=sent_ref,
        dst_ref=back_ref,
        send_sem=back_send,
        recv_sem=back_recv,
        device_id=below,
        device_id_type=MESH,
    )

    def each(action):
        def step(d, _):
            action(d)
            return 0

        lax.fori_loop(1, slabs, step, 0)

    each(lambda d: member_copy(d).start())
    for copy in part_copies:
        copy.start()

    own_loop(ahead_lots, mid_lots)

    member_ref[slab] = group_ref[slab]
    each(lambda d: member_copy(d).wait())
    phi_part(member_ref, phi_ref, energy_ref, phi_target_ref, phi_source_ref)
    each(lambda d: phi_copy(d).start())
    table_ref[slab] = phi_ref[slab]

    for copy in part_copies:
        copy.wait()
    fill(far_parts, plane_ref, far_ref, None, -1.0)
    cross_part(list_ref, dens_ref, column_ref, sent_ref, far_ref, right_ref, near_even_ref, near_odd_ref)
    back_copy.start()

    @pl.when(first_device)
    def _():
        own_run(MID_LOTS + extra, OWN_LOTS - MID_LOTS - extra)

    @pl.when(jnp.logical_not(first_device))
    def _():
        own_run(MID_LOTS, OWN_LOTS - MID_LOTS)

    each(lambda d: phi_copy(d).wait())
    potential_rows(table_ref, count_ref, owner_ref, rest_ref)
    rest_ref[pl.ds(rest_ref.shape[0] - 8, 8), :] = jnp.broadcast_to(energy_ref[...], (8, TILE))
    back_copy.wait()
    dens_ref[...] = (dens_ref[...] + back_ref[...]) * (DENSITY_SCALE / weight_ref[...])


def block_of(parts, i):
    place_ref, mass_ref, size_ref = parts
    row = lax.broadcasted_iota(jnp.int32, (8, TILE), 0)
    block = jnp.broadcast_to(size_ref[pl.ds(i, 1), :], (8, TILE))
    block = jnp.where(row == 3, mass_ref[pl.ds(i, 1), :], block)
    for axis in range(3):
        block = jnp.where(row == axis, place_ref[axis, pl.ds(i, 1), :], block)
    return block


def pick_groups(parts, count_ref, owner_ref, group_ref):
    blocks = parts[1].shape[0]
    row = lax.broadcasted_iota(jnp.int32, (8, TILE), 0)
    lane = lax.broadcasted_iota(jnp.int32, (8, TILE), 1)
    slot = lax.broadcasted_iota(jnp.int32, group_ref.shape, 0)

    def step(k, start):
        count = count_ref[0, k]
        block = jnp.minimum(start // TILE, blocks - 1)
        shift = start % TILE
        first = block_of(parts, block)
        second = block_of(parts, jnp.minimum(block + 1, blocks - 1))
        mixed = pltpu.roll(jnp.where(lane >= shift, first, second), (TILE - shift) % TILE, 1)
        mixed = jnp.where((row == 3) & (lane >= count), 0.0, mixed)
        group_ref[...] = jnp.where(slot == owner_ref[0, k], mixed, group_ref[...])
        return start + count

    group_ref[...] = jnp.zeros_like(group_ref)
    groups = count_ref.shape[1]
    lax.fori_loop(0, groups, step, jnp.int32(0), unroll=math.gcd(groups, 8))


def phi_part(member_ref, phi_ref, energy_ref, target_ref, source_ref):
    slabs = member_ref.shape[0]
    group = math.gcd(slabs, 8)

    def fill(i, _):
        particles = member_ref[i]
        row, coords, norm = centred(particles, 0.0)
        size = particles[4:5]
        norm = norm + 0.125 * size * size
        base = pl.multiple_of(i * TILE, TILE)
        source_ref[:, pl.ds(base, TILE)] = right_rows(
            jnp.where(row < 3, coords, jnp.where(row == 3, norm, jnp.where(row == 4, 1.0, 0.0)))
        )
        target_ref[i] = left_rows(
            jnp.where(row < 3, -2.0 * coords, jnp.where(row == 3, 1.0, jnp.where(row == 4, norm, 0.0)))
        ).T
        return 0

    lax.fori_loop(0, slabs, fill, 0, unroll=group)

    def step(i, energy):
        target = target_ref[i]

        def inner(j, total):
            for n in range(group):
                base = pl.multiple_of((j * group + n) * TILE, TILE)
                pairs = pair_dot(target, source_ref[:, pl.ds(base, TILE)], 1)
                total = total + lax.rsqrt(pairs) * member_ref[j * group + n, 3:4, :]
            return total

        total = lax.fori_loop(0, slabs // group, inner, jnp.zeros((TILE, TILE), F32), unroll=slabs == group)
        mass = member_ref[i, 3:4, :]
        size = member_ref[i, 4:5, :]
        phi = mass * (2.0 / size) - jnp.sum(total.T, axis=0, keepdims=True)
        phi_ref[i] = phi
        return energy + mass * phi

    energy = lax.fori_loop(0, slabs, step, jnp.zeros((1, TILE), F32), unroll=8 if slabs == group else 1)
    energy_ref[...] = 0.5 * jnp.sum(energy, axis=1, keepdims=True)


def potential_rows(table_ref, count_ref, owner_ref, rest_ref):
    groups = count_ref.shape[1]
    used = rest_ref.shape[0] - 8
    rows = pl.ds(0, used)
    rest_ref[rows, :] = jnp.zeros((used, TILE), F32)
    lane = lax.broadcasted_iota(jnp.int32, (used, TILE), 1)
    place = lane + TILE * lax.broadcasted_iota(jnp.int32, (used, TILE), 0)

    def step(k, start):
        count = count_ref[0, k]
        value = pltpu.roll(table_ref[owner_ref[0, k]], start % TILE, 1)
        inside = (place >= start) & (place < start + count)
        rest_ref[rows, :] = jnp.where(inside, value, rest_ref[rows, :])
        return start + count

    lax.fori_loop(0, groups, step, jnp.int32(0), unroll=math.gcd(groups, 8))


def final_kernel(dens_ref, rest_ref, out_ref, pot_ref, energy_ref):
    used = rest_ref.shape[0] - 8
    out_ref[...] = dens_ref[...]
    pot_ref[pl.ds(0, used), :] = rest_ref[pl.ds(0, used), :]
    if used < pot_ref.shape[0]:
        pot_ref[pl.ds(used, pot_ref.shape[0] - used), :] = jnp.zeros((pot_ref.shape[0] - used, TILE), F32)
    energy_ref[...] = rest_ref[pl.ds(used, 1), pl.ds(0, 1)]


def per_device(positions, masses, smoothing, block_lists, block_counts, group_owner):
    row_count = masses.shape[1]
    blocks = row_count // TILE
    slabs = lax.axis_size("slab")
    grps = lax.axis_size("grp")
    particles = (
        positions[0].reshape(3, blocks, TILE),
        masses.reshape(blocks, TILE),
        smoothing.reshape(blocks, TILE),
    )
    grid_shape = jax.ShapeDtypeStruct((blocks, TILE), F32)
    dma = pltpu.SemaphoreType.DMA
    used = min(block_counts.shape[1], blocks)
    density, rest = pl.pallas_call(
        functools.partial(main_kernel, slabs, grps),
        out_shape=(grid_shape, jax.ShapeDtypeStruct((used + 8, TILE), F32)),
        in_specs=[VMEM, VMEM, VMEM, SMEM, SMEM, SMEM],
        out_specs=(VMEM, VMEM),
        scratch_shapes=[
            pltpu.VMEM((slabs, 1, TILE), F32),
            pltpu.VMEM((blocks, TILE), F32),
            pltpu.VMEM((1, 1), F32),
            pltpu.VMEM((3, blocks, TILE), F32),
            pltpu.VMEM((blocks, TILE), F32),
            pltpu.VMEM((blocks, TILE), F32),
            pltpu.VMEM((slabs, 8, TILE), F32),
            pltpu.VMEM((slabs, 8, TILE), F32),
            pltpu.VMEM((slabs, 1, TILE), F32),
            pltpu.VMEM((KX * blocks, TILE), F32),
            pltpu.VMEM((blocks, TILE), F32),
            pltpu.VMEM((blocks, TILE, DEPTH), HALF),
            pltpu.VMEM((blocks, DEPTH, 3 * TILE), HALF),
            pltpu.VMEM((blocks, TILE, DEPTH), HALF),
            pltpu.VMEM((KO * TILE, 3 * TILE), F32),
            pltpu.VMEM((KO * TILE, 3 * TILE), F32),
            pltpu.VMEM((KX * TILE, 3 * TILE), F32),
            pltpu.VMEM((KX * TILE, 3 * TILE), F32),
            pltpu.VMEM((slabs, TILE, 48), HALF),
            pltpu.VMEM((48, slabs * TILE), HALF),
            pltpu.VMEM((PLANES, blocks, TILE), F32),
            dma((slabs,)),
            dma((slabs,)),
            dma((slabs,)),
            dma((slabs,)),
            dma((3,)),
            dma((3,)),
            dma,
            dma,
        ],
        compiler_params=pltpu.CompilerParams(
            collective_id=0,
            has_side_effects=True,
        ),
    )(*particles, block_lists[0].T, block_counts, group_owner)
    density, potential, energy = pl.pallas_call(
        final_kernel,
        out_shape=(grid_shape, grid_shape, jax.ShapeDtypeStruct((1, 1), F32)),
        in_specs=[VMEM, VMEM],
        out_specs=(VMEM, VMEM, VMEM),
    )(density, rest)
    return (density.reshape(1, row_count), potential.reshape(1, row_count), energy)


def solution(mesh):
    placed = (
        P(("slab", "grp"), None, None),
        P(("slab", "grp"), None),
        P(("slab", "grp"), None),
        P(("slab", "grp"), None, None),
        P(("slab", "grp"), None),
        P("grp", None),
    )
    return jax.shard_map(
        per_device,
        mesh=mesh,
        in_specs=placed,
        out_specs=(P(("slab", "grp"), None), P(("slab", "grp"), None), P("grp", "slab")),
        check_vma=False,
    )
```

```python
import functools
import math

import jax
import jax.numpy as jnp
from jax import lax
from jax.experimental import pallas as pl
from jax.experimental.pallas import tpu as pltpu
from jax.sharding import PartitionSpec as P

TILE = 128
KX = 2
KO = 4
F32 = jnp.float32
HALF = jnp.bfloat16
DEPTH = 64
LOT = 8
OWN_LOTS = 8
MID_LOTS = 5

DENSITY_SCALE = 21.0 / (256.0 * math.pi) / 16.0

VMEM = pl.BlockSpec(memory_space=pltpu.VMEM)
MESH = pl.DeviceIdType.MESH
SMEM = pl.BlockSpec(memory_space=pltpu.SMEM)


def split3(a):
    high = a.astype(HALF).astype(F32)
    rest = a - high
    mid = rest.astype(HALF).astype(F32)
    return high, mid, rest - mid


def left_six(a):
    high, mid, low = split3(a)
    return [high, high, mid, high, low, mid]


def right_six(a):
    high, mid, low = split3(a)
    return [high, mid, high, low, high, mid]


def left_rows(a):
    return jnp.concatenate(left_six(a), axis=0).astype(HALF)


def right_rows(a):
    return jnp.concatenate(right_six(a), axis=0).astype(HALF)


def centred(particles, lift):
    row = lax.broadcasted_iota(jnp.int32, particles.shape, 0)
    shift = jnp.where(row == 0, lift - 0.5, jnp.where(row < 3, -0.5, 0.0))
    coords = jnp.where(row < 3, particles + shift, 0.0)
    norm = jnp.sum(coords * coords, axis=0, keepdims=True)
    return row, coords, norm


FACTORS = 8
NORM, SIZE, PLANES = 8, 11, 14


def fill_planes(parts, plane_ref, lift):
    place_ref, mass_ref, size_ref = parts

    def step(i, _):
        rows = pl.ds(pl.multiple_of(i * LOT, LOT), LOT)
        coords = [place_ref[axis, rows, :] + ((lift if axis == 0 else 0.0) - 0.5) for axis in range(3)]
        norm = coords[0] * coords[0] + coords[1] * coords[1] + coords[2] * coords[2]
        size = size_ref[rows, :]
        planes = coords + [lax.rsqrt(mass_ref[rows, :])]
        for _ in range(4):
            planes.append(planes[-1] * size)
        planes += list(split3(norm)) + list(split3(size))
        for n, plane in enumerate(planes):
            plane_ref[n, rows, :] = plane
        return 0

    lax.fori_loop(0, mass_ref.shape[0] // LOT, step, 0, unroll=2)


def by_row(values):
    row = lax.broadcasted_iota(jnp.int32, (8, TILE), 0)
    block = jnp.broadcast_to(values[0], (8, TILE))
    for n, value in enumerate(values[1:]):
        block = jnp.where(row == n + 1, value, block)
    return block


def fill(parts, plane_ref, left_ref, right_ref, lift):
    fill_planes(parts, plane_ref, lift)
    row = lax.broadcasted_iota(jnp.int32, (8, TILE), 0)
    zero = jnp.zeros((8, TILE), F32)

    def step(i, _):
        plane = [plane_ref[n, pl.ds(i, 1), :] for n in range(PLANES)]
        coords, powers, norm, size = plane[:3], plane[3:8], plane[NORM:SIZE], plane[SIZE:]
        high, mid, low = split3(by_row(coords + powers[::-1]))
        rest = by_row(norm + [1.0, 1.0, 1.0] + size[:2])
        last = jnp.where(row == 0, size[2], 0.0)
        left_ref[i] = jnp.concatenate([high, high, high, mid, mid, low, rest, last], axis=0).astype(HALF).T
        if right_ref is not None:
            scale = by_row([-8.0, -8.0, -8.0, 0.0625, 0.25, 0.375, 0.25, 0.0625])
            parts3 = split3(scale * by_row(coords + powers))
            near = [jnp.where(row < 3, part, 0.0) for part in parts3]
            far = [jnp.where(row < 3, 0.0, part) for part in parts3]
            order = (0, 1, 2, 0, 1, 0)
            rest = by_row([4.0, 4.0, 4.0] + [4.0 * part for part in norm] + [0.0, 0.0])
            wide = by_row([0.0, 0.0, 0.0] + [2.0 * part for part in size] + [2.0, 2.0])
            last = jnp.where(row == 0, 2.0, 0.0)
            columns = (
                [near[n] for n in order] + [rest, zero],
                [zero] * 6 + [wide, last],
                [far[n] for n in order] + [zero, zero],
            )
            for m, column in enumerate(columns):
                right_ref[i, :, pl.ds(m * TILE, TILE)] = jnp.concatenate(column, axis=0).astype(HALF)
        return 0

    lax.fori_loop(0, left_ref.shape[0], step, 0, unroll=16)


def pair_dot(left, right, left_dim=0):
    return lax.dot_general(
        left, right, (((left_dim,), (0,)), ((), ())), preferred_element_type=F32
    )


def weights(both_ref, base):
    rows = pl.ds(base, 8)
    squared = jnp.maximum(both_ref[rows, :TILE], 1e-30)
    reach = both_ref[rows, TILE : 2 * TILE]
    near = jnp.maximum(reach - squared * lax.rsqrt(squared), 0.0)
    a = near * lax.rsqrt(both_ref[rows, 2 * TILE : 3 * TILE])
    a = a * a
    return (a * a) * (1.25 * reach - near)


def sweep(first, steps, end, fetch, use, even_ref, odd_ref, unroll):
    def step(i, _):
        b = first + 2 * i
        fetch(b + 1, odd_ref)
        use(b, even_ref)
        fetch(jnp.minimum(b + 2, end - 1), even_ref)
        use(b + 1, odd_ref)
        return 0

    lax.fori_loop(0, steps, step, 0, unroll=unroll)


def own_part(list_ref, dens_ref, left_ref, right_ref, even_ref, odd_ref):
    blocks = left_ref.shape[0]
    lot = blocks // OWN_LOTS

    def fetch(b, both_ref):
        right = right_ref[b]
        for k in range(KO):
            both_ref[pl.ds(k * TILE, TILE), :] = pair_dot(left_ref[list_ref[KX + k, b]], right, 1)

    def use(b, both_ref):
        total = jnp.zeros((8, TILE), F32)
        for base in range(0, KO * TILE, 8):
            total = total + weights(both_ref, base)
        dens_ref[pl.ds(b, 1), :] += jnp.sum(total, axis=0, keepdims=True)

    def run(first, lots):
        steps = lots * lot // 2
        sweep(first * lot, steps, blocks, fetch, use, even_ref, odd_ref, steps)

    def loop(first, last):
        def one(i, _):
            run(i, 1)
            return 0

        lax.fori_loop(first, last, one, 0)

    return functools.partial(fetch, 0, even_ref), loop, run


def cross_part(list_ref, dens_ref, column_ref, back_ref, far_ref, right_ref, even_ref, odd_ref):
    blocks = far_ref.shape[0]

    def fetch(b, both_ref):
        left = jnp.concatenate([far_ref[list_ref[k, b]] for k in range(KX)], axis=0)
        both_ref[...] = pair_dot(left, right_ref[b], 1)

    def use(b, both_ref):
        total = jnp.zeros((8, TILE), F32)
        for k in range(KX):
            values = [weights(both_ref, k * TILE + base) for base in range(0, TILE, 8)]
            for value in values:
                total = total + value
            column = jnp.concatenate(values, axis=0).T
            column_ref[pl.ds(KX * b + k, 1), :] = jnp.sum(column, axis=0, keepdims=True)
        dens_ref[pl.ds(b, 1), :] += jnp.sum(total, axis=0, keepdims=True)

    fetch(0, even_ref)
    sweep(0, blocks // 2, blocks, fetch, use, even_ref, odd_ref, math.gcd(blocks // 2, 16))

    lane = lax.broadcasted_iota(jnp.int32, (1, KX * blocks), 1)

    def name(b, row):
        for k in range(KX):
            row = jnp.where(lane == KX * b + k, list_ref[k, b], row)
        return row

    named = lax.fori_loop(0, blocks, name, jnp.zeros((1, KX * blocks), jnp.int32), unroll=8)
    block = lax.broadcasted_iota(jnp.int32, (blocks, KX * blocks), 0)
    chosen = jnp.where(block == named, 1.0, 0.0).astype(HALF)
    high, mid, low = split3(column_ref[...])
    back_ref[...] = sum(
        jnp.dot(chosen, part.astype(HALF), preferred_element_type=F32) for part in (low, mid, high)
    )


def main_kernel(
    slabs,
    grps,
    place_ref,
    weight_ref,
    size_ref,
    list_ref,
    count_ref,
    owner_ref,
    dens_ref,
    rest_ref,
    table_ref,
    back_ref,
    energy_ref,
    far_place_ref,
    far_weight_ref,
    far_size_ref,
    group_ref,
    member_ref,
    phi_ref,
    column_ref,
    sent_ref,
    left_ref,
    right_ref,
    far_ref,
    even_ref,
    odd_ref,
    near_even_ref,
    near_odd_ref,
    phi_target_ref,
    phi_source_ref,
    plane_ref,
    member_send,
    member_recv,
    phi_send,
    phi_recv,
    part_send,
    part_recv,
    back_send,
    back_recv,
):
    slab = lax.axis_index("slab")
    grp = lax.axis_index("grp")
    count = slabs * grps
    here = slab * grps + grp

    def place(index):
        return (index // grps, lax.rem(index, grps))

    above = place(lax.rem(here + 1, count))
    below = place(lax.rem(here + count - 1, count))

    def ahead(d):
        return lax.rem(slab + d, slabs)

    barrier = pltpu.get_barrier_semaphore()
    for other in (above, below):
        pl.semaphore_signal(barrier, inc=1, device_id=other, device_id_type=MESH)

    def greet(d, _):
        pl.semaphore_signal(barrier, inc=1, device_id=(ahead(d), grp), device_id_type=MESH)
        return 0

    lax.fori_loop(1, slabs, greet, 0)
    parts = (place_ref, weight_ref, size_ref)
    far_parts = (far_place_ref, far_weight_ref, far_size_ref)
    blocks = dens_ref.shape[0]
    first_device = here < count // 32
    ahead_lots = sum((here < count * n // 32).astype(jnp.int32) for n in (1, 1, 4, 20))
    extra = OWN_LOTS - 1 - MID_LOTS
    mid_lots = MID_LOTS + extra * first_device.astype(jnp.int32)
    prepare_own, own_loop, own_run = own_part(list_ref, dens_ref, left_ref, right_ref, even_ref, odd_ref)
    dens_ref[...] = jnp.zeros_like(dens_ref)
    fill(parts, plane_ref, left_ref, right_ref, 0.0)
    pick_groups(parts, count_ref, owner_ref, group_ref)
    prepare_own()
    own_loop(0, ahead_lots)
    pl.semaphore_wait(barrier, slabs + 1)

    def member_copy(d):
        return pltpu.make_async_remote_copy(
            src_ref=group_ref.at[ahead(d)],
            dst_ref=member_ref.at[slab],
            send_sem=member_send.at[d],
            recv_sem=member_recv.at[d],
            device_id=(ahead(d), grp),
            device_id_type=MESH,
        )

    def phi_copy(d):
        return pltpu.make_async_remote_copy(
            src_ref=phi_ref.at[ahead(d)],
            dst_ref=table_ref.at[slab],
            send_sem=phi_send.at[d],
            recv_sem=phi_recv.at[d],
            device_id=(ahead(d), grp),
            device_id_type=MESH,
        )

    part_copies = [
        pltpu.make_async_remote_copy(
            src_ref=near,
            dst_ref=far,
            send_sem=part_send.at[n],
            recv_sem=part_recv.at[n],
            device_id=above,
            device_id_type=MESH,
        )
        for n, (near, far) in enumerate(zip(parts, far_parts))
    ]
    back_copy = pltpu.make_async_remote_copy(
        src_ref=sent_ref,
        dst_ref=back_ref,
        send_sem=back_send,
        recv_sem=back_recv,
        device_id=below,
        device_id_type=MESH,
    )

    def each(action):
        def step(d, _):
            action(d)
            return 0

        lax.fori_loop(1, slabs, step, 0)

    each(lambda d: member_copy(d).start())
    for copy in part_copies:
        copy.start()

    own_loop(ahead_lots, mid_lots)

    member_ref[slab] = group_ref[slab]
    each(lambda d: member_copy(d).wait())
    phi_part(member_ref, phi_ref, energy_ref, phi_target_ref, phi_source_ref)
    each(lambda d: phi_copy(d).start())
    table_ref[slab] = phi_ref[slab]

    for copy in part_copies:
        copy.wait()
    fill(far_parts, plane_ref, far_ref, None, -1.0)
    cross_part(list_ref, dens_ref, column_ref, sent_ref, far_ref, right_ref, near_even_ref, near_odd_ref)
    back_copy.start()

    @pl.when(first_device)
    def _():
        own_run(MID_LOTS + extra, OWN_LOTS - MID_LOTS - extra)

    @pl.when(jnp.logical_not(first_device))
    def _():
        own_run(MID_LOTS, OWN_LOTS - MID_LOTS)

    each(lambda d: phi_copy(d).wait())
    potential_rows(table_ref, count_ref, owner_ref, rest_ref)
    rest_ref[pl.ds(rest_ref.shape[0] - 8, 8), :] = jnp.broadcast_to(energy_ref[...], (8, TILE))
    back_copy.wait()
    dens_ref[...] = (dens_ref[...] + back_ref[...]) * (DENSITY_SCALE / weight_ref[...])


def block_of(parts, i):
    place_ref, mass_ref, size_ref = parts
    row = lax.broadcasted_iota(jnp.int32, (8, TILE), 0)
    block = jnp.broadcast_to(size_ref[pl.ds(i, 1), :], (8, TILE))
    block = jnp.where(row == 3, mass_ref[pl.ds(i, 1), :], block)
    for axis in range(3):
        block = jnp.where(row == axis, place_ref[axis, pl.ds(i, 1), :], block)
    return block


def pick_groups(parts, count_ref, owner_ref, group_ref):
    blocks = parts[1].shape[0]
    row = lax.broadcasted_iota(jnp.int32, (8, TILE), 0)
    lane = lax.broadcasted_iota(jnp.int32, (8, TILE), 1)
    slot = lax.broadcasted_iota(jnp.int32, group_ref.shape, 0)

    def step(k, start):
        count = count_ref[0, k]
        block = jnp.minimum(start // TILE, blocks - 1)
        shift = start % TILE
        first = block_of(parts, block)
        second = block_of(parts, jnp.minimum(block + 1, blocks - 1))
        mixed = pltpu.roll(jnp.where(lane >= shift, first, second), (TILE - shift) % TILE, 1)
        mixed = jnp.where((row == 3) & (lane >= count), 0.0, mixed)
        group_ref[...] = jnp.where(slot == owner_ref[0, k], mixed, group_ref[...])
        return start + count

    group_ref[...] = jnp.zeros_like(group_ref)
    groups = count_ref.shape[1]
    lax.fori_loop(0, groups, step, jnp.int32(0), unroll=math.gcd(groups, 8))


def phi_part(member_ref, phi_ref, energy_ref, target_ref, source_ref):
    slabs = member_ref.shape[0]
    group = math.gcd(slabs, 8)

    def fill(i, _):
        particles = member_ref[i]
        row, coords, norm = centred(particles, 0.0)
        size = particles[4:5]
        norm = norm + 0.125 * size * size
        base = pl.multiple_of(i * TILE, TILE)
        source_ref[:, pl.ds(base, TILE)] = right_rows(
            jnp.where(row < 3, coords, jnp.where(row == 3, norm, jnp.where(row == 4, 1.0, 0.0)))
        )
        target_ref[i] = left_rows(
            jnp.where(row < 3, -2.0 * coords, jnp.where(row == 3, 1.0, jnp.where(row == 4, norm, 0.0)))
        ).T
        return 0

    lax.fori_loop(0, slabs, fill, 0, unroll=group)

    def step(i, energy):
        target = target_ref[i]

        def inner(j, total):
            for n in range(group):
                base = pl.multiple_of((j * group + n) * TILE, TILE)
                pairs = pair_dot(target, source_ref[:, pl.ds(base, TILE)], 1)
                total = total + lax.rsqrt(pairs) * member_ref[j * group + n, 3:4, :]
            return total

        total = lax.fori_loop(0, slabs // group, inner, jnp.zeros((TILE, TILE), F32), unroll=slabs == group)
        mass = member_ref[i, 3:4, :]
        size = member_ref[i, 4:5, :]
        phi = mass * (2.0 / size) - jnp.sum(total.T, axis=0, keepdims=True)
        phi_ref[i] = phi
        return energy + mass * phi

    energy = lax.fori_loop(0, slabs, step, jnp.zeros((1, TILE), F32), unroll=8 if slabs == group else 1)
    energy_ref[...] = 0.5 * jnp.sum(energy, axis=1, keepdims=True)


def potential_rows(table_ref, count_ref, owner_ref, rest_ref):
    groups = count_ref.shape[1]
    used = rest_ref.shape[0] - 8
    rows = pl.ds(0, used)
    rest_ref[rows, :] = jnp.zeros((used, TILE), F32)
    lane = lax.broadcasted_iota(jnp.int32, (used, TILE), 1)
    place = lane + TILE * lax.broadcasted_iota(jnp.int32, (used, TILE), 0)

    def step(k, start):
        count = count_ref[0, k]
        value = pltpu.roll(table_ref[owner_ref[0, k]], start % TILE, 1)
        inside = (place >= start) & (place < start + count)
        rest_ref[rows, :] = jnp.where(inside, value, rest_ref[rows, :])
        return start + count

    lax.fori_loop(0, groups, step, jnp.int32(0), unroll=math.gcd(groups, 8))


def final_kernel(dens_ref, rest_ref, out_ref, pot_ref, energy_ref):
    used = rest_ref.shape[0] - 8
    out_ref[...] = dens_ref[...]
    pot_ref[pl.ds(0, used), :] = rest_ref[pl.ds(0, used), :]
    if used < pot_ref.shape[0]:
        pot_ref[pl.ds(used, pot_ref.shape[0] - used), :] = jnp.zeros((pot_ref.shape[0] - used, TILE), F32)
    energy_ref[...] = rest_ref[pl.ds(used, 1), pl.ds(0, 1)]


def per_device(positions, masses, smoothing, block_lists, block_counts, group_owner):
    row_count = masses.shape[1]
    blocks = row_count // TILE
    slabs = lax.axis_size("slab")
    grps = lax.axis_size("grp")
    particles = (
        positions[0].reshape(3, blocks, TILE),
        masses.reshape(blocks, TILE),
        smoothing.reshape(blocks, TILE),
    )
    grid_shape = jax.ShapeDtypeStruct((blocks, TILE), F32)
    dma = pltpu.SemaphoreType.DMA
    used = min(block_counts.shape[1], blocks)
    density, rest = pl.pallas_call(
        functools.partial(main_kernel, slabs, grps),
        out_shape=(grid_shape, jax.ShapeDtypeStruct((used + 8, TILE), F32)),
        in_specs=[VMEM, VMEM, VMEM, SMEM, SMEM, SMEM],
        out_specs=(VMEM, VMEM),
        scratch_shapes=[
            pltpu.VMEM((slabs, 1, TILE), F32),
            pltpu.VMEM((blocks, TILE), F32),
            pltpu.VMEM((1, 1), F32),
            pltpu.VMEM((3, blocks, TILE), F32),
            pltpu.VMEM((blocks, TILE), F32),
            pltpu.VMEM((blocks, TILE), F32),
            pltpu.VMEM((slabs, 8, TILE), F32),
            pltpu.VMEM((slabs, 8, TILE), F32),
            pltpu.VMEM((slabs, 1, TILE), F32),
            pltpu.VMEM((KX * blocks, TILE), F32),
            pltpu.VMEM((blocks, TILE), F32),
            pltpu.VMEM((blocks, TILE, DEPTH), HALF),
            pltpu.VMEM((blocks, DEPTH, 3 * TILE), HALF),
            pltpu.VMEM((blocks, TILE, DEPTH), HALF),
            pltpu.VMEM((KO * TILE, 3 * TILE), F32),
            pltpu.VMEM((KO * TILE, 3 * TILE), F32),
            pltpu.VMEM((KX * TILE, 3 * TILE), F32),
            pltpu.VMEM((KX * TILE, 3 * TILE), F32),
            pltpu.VMEM((slabs, TILE, 48), HALF),
            pltpu.VMEM((48, slabs * TILE), HALF),
            pltpu.VMEM((PLANES, blocks, TILE), F32),
            dma((slabs,)),
            dma((slabs,)),
            dma((slabs,)),
            dma((slabs,)),
            dma((3,)),
            dma((3,)),
            dma,
            dma,
        ],
        compiler_params=pltpu.CompilerParams(
            collective_id=0,
            has_side_effects=True,
        ),
    )(*particles, block_lists[0].T, block_counts, group_owner)
    density, potential, energy = pl.pallas_call(
        final_kernel,
        out_shape=(grid_shape, grid_shape, jax.ShapeDtypeStruct((1, 1), F32)),
        in_specs=[VMEM, VMEM],
        out_specs=(VMEM, VMEM, VMEM),
    )(density, rest)
    return (density.reshape(1, row_count), potential.reshape(1, row_count), energy)


def solution(mesh):
    placed = (
        P(("slab", "grp"), None, None),
        P(("slab", "grp"), None),
        P(("slab", "grp"), None),
        P(("slab", "grp"), None, None),
        P(("slab", "grp"), None),
        P("grp", None),
    )
    return jax.shard_map(
        per_device,
        mesh=mesh,
        in_specs=placed,
        out_specs=(P(("slab", "grp"), None), P(("slab", "grp"), None), P("grp", "slab")),
        check_vma=False,
    )
```

```python
import functools
import math

import jax
import jax.numpy as jnp
from jax import lax
from jax.experimental import pallas as pl
from jax.experimental.pallas import tpu as pltpu
from jax.sharding import PartitionSpec as P

TILE = 128
KX = 2
KO = 4
F32 = jnp.float32
HALF = jnp.bfloat16
DEPTH = 64
LOT = 8
OWN_LOTS = 8
MID_LOTS = 5

DENSITY_SCALE = 21.0 / (256.0 * math.pi) / 16.0

VMEM = pl.BlockSpec(memory_space=pltpu.VMEM)
ANY = pl.BlockSpec(memory_space=pl.ANY)
MESH = pl.DeviceIdType.MESH
SMEM = pl.BlockSpec(memory_space=pltpu.SMEM)


def split3(a):
    high = a.astype(HALF).astype(F32)
    rest = a - high
    mid = rest.astype(HALF).astype(F32)
    return high, mid, rest - mid


def left_six(a):
    high, mid, low = split3(a)
    return [high, high, mid, high, low, mid]


def right_six(a):
    high, mid, low = split3(a)
    return [high, mid, high, low, high, mid]


def left_rows(a):
    return jnp.concatenate(left_six(a), axis=0).astype(HALF)


def right_rows(a):
    return jnp.concatenate(right_six(a), axis=0).astype(HALF)


def centred(particles, lift):
    row = lax.broadcasted_iota(jnp.int32, particles.shape, 0)
    shift = jnp.where(row == 0, lift - 0.5, jnp.where(row < 3, -0.5, 0.0))
    coords = jnp.where(row < 3, particles + shift, 0.0)
    norm = jnp.sum(coords * coords, axis=0, keepdims=True)
    return row, coords, norm


FACTORS = 8
NORM, SIZE, PLANES = 8, 11, 14


def fill_planes(parts, plane_ref, lift):
    place_ref, mass_ref, size_ref = parts

    def step(i, _):
        rows = pl.ds(pl.multiple_of(i * LOT, LOT), LOT)
        coords = [place_ref[axis, rows, :] + ((lift if axis == 0 else 0.0) - 0.5) for axis in range(3)]
        norm = coords[0] * coords[0] + coords[1] * coords[1] + coords[2] * coords[2]
        size = size_ref[rows, :]
        planes = coords + [lax.rsqrt(mass_ref[rows, :])]
        for _ in range(4):
            planes.append(planes[-1] * size)
        planes += list(split3(norm)) + list(split3(size))
        for n, plane in enumerate(planes):
            plane_ref[n, rows, :] = plane
        return 0

    lax.fori_loop(0, mass_ref.shape[0] // LOT, step, 0, unroll=2)


def by_row(values):
    row = lax.broadcasted_iota(jnp.int32, (8, TILE), 0)
    block = jnp.broadcast_to(values[0], (8, TILE))
    for n, value in enumerate(values[1:]):
        block = jnp.where(row == n + 1, value, block)
    return block


def fill(parts, plane_ref, left_ref, right_ref, lift):
    fill_planes(parts, plane_ref, lift)
    row = lax.broadcasted_iota(jnp.int32, (8, TILE), 0)
    zero = jnp.zeros((8, TILE), F32)

    def step(i, _):
        plane = [plane_ref[n, pl.ds(i, 1), :] for n in range(PLANES)]
        coords, powers, norm, size = plane[:3], plane[3:8], plane[NORM:SIZE], plane[SIZE:]
        high, mid, low = split3(by_row(coords + powers[::-1]))
        rest = by_row(norm + [1.0, 1.0, 1.0] + size[:2])
        last = jnp.where(row == 0, size[2], 0.0)
        left_ref[i] = jnp.concatenate([high, high, high, mid, mid, low, rest, last], axis=0).astype(HALF).T
        if right_ref is not None:
            scale = by_row([-8.0, -8.0, -8.0, 0.0625, 0.25, 0.375, 0.25, 0.0625])
            parts3 = split3(scale * by_row(coords + powers))
            near = [jnp.where(row < 3, part, 0.0) for part in parts3]
            far = [jnp.where(row < 3, 0.0, part) for part in parts3]
            order = (0, 1, 2, 0, 1, 0)
            rest = by_row([4.0, 4.0, 4.0] + [4.0 * part for part in norm] + [0.0, 0.0])
            wide = by_row([0.0, 0.0, 0.0] + [2.0 * part for part in size] + [2.0, 2.0])
            last = jnp.where(row == 0, 2.0, 0.0)
            columns = (
                [near[n] for n in order] + [rest, zero],
                [zero] * 6 + [wide, last],
                [far[n] for n in order] + [zero, zero],
            )
            for m, column in enumerate(columns):
                right_ref[i, :, pl.ds(m * TILE, TILE)] = jnp.concatenate(column, axis=0).astype(HALF)
        return 0

    lax.fori_loop(0, left_ref.shape[0], step, 0, unroll=16)


def pair_dot(left, right, left_dim=0):
    return lax.dot_general(
        left, right, (((left_dim,), (0,)), ((), ())), preferred_element_type=F32
    )


def weights(both_ref, base):
    rows = pl.ds(base, 8)
    squared = jnp.maximum(both_ref[rows, :TILE], 1e-30)
    reach = both_ref[rows, TILE : 2 * TILE]
    near = jnp.maximum(reach - squared * lax.rsqrt(squared), 0.0)
    a = near * lax.rsqrt(both_ref[rows, 2 * TILE : 3 * TILE])
    a = a * a
    return (a * a) * (1.25 * reach - near)


def sweep(first, steps, end, fetch, use, even_ref, odd_ref, unroll):
    def step(i, _):
        b = first + 2 * i
        fetch(b + 1, odd_ref)
        use(b, even_ref)
        fetch(jnp.minimum(b + 2, end - 1), even_ref)
        use(b + 1, odd_ref)
        return 0

    lax.fori_loop(0, steps, step, 0, unroll=unroll)


def own_part(list_ref, dens_ref, left_ref, right_ref, even_ref, odd_ref):
    blocks = left_ref.shape[0]
    lot = blocks // OWN_LOTS

    def fetch(b, both_ref):
        right = right_ref[b]
        for k in range(KO):
            both_ref[pl.ds(k * TILE, TILE), :] = pair_dot(left_ref[list_ref[KX + k, b]], right, 1)

    def use(b, both_ref):
        total = jnp.zeros((8, TILE), F32)
        for base in range(0, KO * TILE, 8):
            total = total + weights(both_ref, base)
        dens_ref[pl.ds(b, 1), :] += jnp.sum(total, axis=0, keepdims=True)

    def run(first, lots):
        steps = lots * lot // 2
        sweep(first * lot, steps, blocks, fetch, use, even_ref, odd_ref, steps)

    def loop(first, last):
        def one(i, _):
            run(i, 1)
            return 0

        lax.fori_loop(first, last, one, 0)

    return functools.partial(fetch, 0, even_ref), loop, run


def cross_part(list_ref, dens_ref, column_ref, back_ref, far_ref, right_ref, even_ref, odd_ref):
    blocks = far_ref.shape[0]

    def fetch(b, both_ref):
        left = jnp.concatenate([far_ref[list_ref[k, b]] for k in range(KX)], axis=0)
        both_ref[...] = pair_dot(left, right_ref[b], 1)

    def use(b, both_ref):
        total = jnp.zeros((8, TILE), F32)
        for k in range(KX):
            values = [weights(both_ref, k * TILE + base) for base in range(0, TILE, 8)]
            for value in values:
                total = total + value
            column = jnp.concatenate(values, axis=0).T
            column_ref[pl.ds(KX * b + k, 1), :] = jnp.sum(column, axis=0, keepdims=True)
        dens_ref[pl.ds(b, 1), :] += jnp.sum(total, axis=0, keepdims=True)

    fetch(0, even_ref)
    sweep(0, blocks // 2, blocks, fetch, use, even_ref, odd_ref, math.gcd(blocks // 2, 16))

    lane = lax.broadcasted_iota(jnp.int32, (1, KX * blocks), 1)

    def name(b, row):
        for k in range(KX):
            row = jnp.where(lane == KX * b + k, list_ref[k, b], row)
        return row

    named = lax.fori_loop(0, blocks, name, jnp.zeros((1, KX * blocks), jnp.int32), unroll=8)
    block = lax.broadcasted_iota(jnp.int32, (blocks, KX * blocks), 0)
    chosen = jnp.where(block == named, 1.0, 0.0).astype(HALF)
    high, mid, low = split3(column_ref[...])
    back_ref[...] = sum(
        jnp.dot(chosen, part.astype(HALF), preferred_element_type=F32) for part in (low, mid, high)
    )


def main_kernel(
    slabs,
    grps,
    place_in_ref,
    weight_in_ref,
    size_in_ref,
    list_ref,
    count_ref,
    owner_ref,
    dens_ref,
    rest_ref,
    table_ref,
    back_ref,
    energy_ref,
    place_ref,
    weight_ref,
    size_ref,
    far_place_ref,
    far_weight_ref,
    far_size_ref,
    group_ref,
    member_ref,
    phi_ref,
    column_ref,
    sent_ref,
    left_ref,
    right_ref,
    far_ref,
    even_ref,
    odd_ref,
    near_even_ref,
    near_odd_ref,
    phi_target_ref,
    phi_source_ref,
    plane_ref,
    load_sem,
    member_send,
    member_recv,
    phi_send,
    phi_recv,
    part_send,
    part_recv,
    back_send,
    back_recv,
):
    slab = lax.axis_index("slab")
    grp = lax.axis_index("grp")
    count = slabs * grps
    here = slab * grps + grp

    def place(index):
        return (index // grps, lax.rem(index, grps))

    above = place(lax.rem(here + 1, count))
    below = place(lax.rem(here + count - 1, count))

    def ahead(d):
        return lax.rem(slab + d, slabs)

    barrier = pltpu.get_barrier_semaphore()
    for other in (above, below):
        pl.semaphore_signal(barrier, inc=1, device_id=other, device_id_type=MESH)

    def greet(d, _):
        pl.semaphore_signal(barrier, inc=1, device_id=(ahead(d), grp), device_id_type=MESH)
        return 0

    lax.fori_loop(1, slabs, greet, 0)
    parts = (place_ref, weight_ref, size_ref)
    far_parts = (far_place_ref, far_weight_ref, far_size_ref)
    loads = [
        pltpu.make_async_copy(source, part, load_sem.at[n])
        for n, (source, part) in enumerate(zip((place_in_ref, weight_in_ref, size_in_ref), parts))
    ]
    for load in loads:
        load.start()
    blocks = dens_ref.shape[0]
    first_device = here < count // 32
    ahead_lots = sum((here < count * n // 32).astype(jnp.int32) for n in (1, 1, 4, 20))
    extra = OWN_LOTS - 1 - MID_LOTS
    mid_lots = MID_LOTS + extra * first_device.astype(jnp.int32)
    prepare_own, own_loop, own_run = own_part(list_ref, dens_ref, left_ref, right_ref, even_ref, odd_ref)
    dens_ref[...] = jnp.zeros_like(dens_ref)
    for load in loads:
        load.wait()
    fill(parts, plane_ref, left_ref, right_ref, 0.0)
    pick_groups(parts, count_ref, owner_ref, group_ref)
    prepare_own()
    own_loop(0, ahead_lots)
    pl.semaphore_wait(barrier, slabs + 1)

    def member_copy(d):
        return pltpu.make_async_remote_copy(
            src_ref=group_ref.at[ahead(d)],
            dst_ref=member_ref.at[slab],
            send_sem=member_send.at[d],
            recv_sem=member_recv.at[d],
            device_id=(ahead(d), grp),
            device_id_type=MESH,
        )

    def phi_copy(d):
        return pltpu.make_async_remote_copy(
            src_ref=phi_ref.at[ahead(d)],
            dst_ref=table_ref.at[slab],
            send_sem=phi_send.at[d],
            recv_sem=phi_recv.at[d],
            device_id=(ahead(d), grp),
            device_id_type=MESH,
        )

    part_copies = [
        pltpu.make_async_remote_copy(
            src_ref=near,
            dst_ref=far,
            send_sem=part_send.at[n],
            recv_sem=part_recv.at[n],
            device_id=above,
            device_id_type=MESH,
        )
        for n, (near, far) in enumerate(zip(parts, far_parts))
    ]
    back_copy = pltpu.make_async_remote_copy(
        src_ref=sent_ref,
        dst_ref=back_ref,
        send_sem=back_send,
        recv_sem=back_recv,
        device_id=below,
        device_id_type=MESH,
    )

    def each(action):
        def step(d, _):
            action(d)
            return 0

        lax.fori_loop(1, slabs, step, 0)

    each(lambda d: member_copy(d).start())
    for copy in part_copies:
        copy.start()

    own_loop(ahead_lots, mid_lots)

    member_ref[slab] = group_ref[slab]
    each(lambda d: member_copy(d).wait())
    phi_part(member_ref, phi_ref, energy_ref, phi_target_ref, phi_source_ref)
    each(lambda d: phi_copy(d).start())
    table_ref[slab] = phi_ref[slab]

    for copy in part_copies:
        copy.wait()
    fill(far_parts, plane_ref, far_ref, None, -1.0)
    cross_part(list_ref, dens_ref, column_ref, sent_ref, far_ref, right_ref, near_even_ref, near_odd_ref)
    back_copy.start()

    @pl.when(first_device)
    def _():
        own_run(MID_LOTS + extra, OWN_LOTS - MID_LOTS - extra)

    @pl.when(jnp.logical_not(first_device))
    def _():
        own_run(MID_LOTS, OWN_LOTS - MID_LOTS)

    each(lambda d: phi_copy(d).wait())
    potential_rows(table_ref, count_ref, owner_ref, rest_ref)
    rest_ref[pl.ds(rest_ref.shape[0] - 8, 8), :] = jnp.broadcast_to(energy_ref[...], (8, TILE))
    back_copy.wait()
    dens_ref[...] = (dens_ref[...] + back_ref[...]) * (DENSITY_SCALE / weight_ref[...])


def block_of(parts, i):
    place_ref, mass_ref, size_ref = parts
    row = lax.broadcasted_iota(jnp.int32, (8, TILE), 0)
    block = jnp.broadcast_to(size_ref[pl.ds(i, 1), :], (8, TILE))
    block = jnp.where(row == 3, mass_ref[pl.ds(i, 1), :], block)
    for axis in range(3):
        block = jnp.where(row == axis, place_ref[axis, pl.ds(i, 1), :], block)
    return block


def pick_groups(parts, count_ref, owner_ref, group_ref):
    blocks = parts[1].shape[0]
    row = lax.broadcasted_iota(jnp.int32, (8, TILE), 0)
    lane = lax.broadcasted_iota(jnp.int32, (8, TILE), 1)
    slot = lax.broadcasted_iota(jnp.int32, group_ref.shape, 0)

    def step(k, start):
        count = count_ref[0, k]
        block = jnp.minimum(start // TILE, blocks - 1)
        shift = start % TILE
        first = block_of(parts, block)
        second = block_of(parts, jnp.minimum(block + 1, blocks - 1))
        mixed = pltpu.roll(jnp.where(lane >= shift, first, second), (TILE - shift) % TILE, 1)
        mixed = jnp.where((row == 3) & (lane >= count), 0.0, mixed)
        group_ref[...] = jnp.where(slot == owner_ref[0, k], mixed, group_ref[...])
        return start + count

    group_ref[...] = jnp.zeros_like(group_ref)
    groups = count_ref.shape[1]
    lax.fori_loop(0, groups, step, jnp.int32(0), unroll=math.gcd(groups, 8))


def phi_part(member_ref, phi_ref, energy_ref, target_ref, source_ref):
    slabs = member_ref.shape[0]
    group = math.gcd(slabs, 8)

    def fill(i, _):
        particles = member_ref[i]
        row, coords, norm = centred(particles, 0.0)
        size = particles[4:5]
        norm = norm + 0.125 * size * size
        base = pl.multiple_of(i * TILE, TILE)
        source_ref[:, pl.ds(base, TILE)] = right_rows(
            jnp.where(row < 3, coords, jnp.where(row == 3, norm, jnp.where(row == 4, 1.0, 0.0)))
        )
        target_ref[i] = left_rows(
            jnp.where(row < 3, -2.0 * coords, jnp.where(row == 3, 1.0, jnp.where(row == 4, norm, 0.0)))
        ).T
        return 0

    lax.fori_loop(0, slabs, fill, 0, unroll=group)

    def step(i, energy):
        target = target_ref[i]

        def inner(j, total):
            for n in range(group):
                base = pl.multiple_of((j * group + n) * TILE, TILE)
                pairs = pair_dot(target, source_ref[:, pl.ds(base, TILE)], 1)
                total = total + lax.rsqrt(pairs) * member_ref[j * group + n, 3:4, :]
            return total

        total = lax.fori_loop(0, slabs // group, inner, jnp.zeros((TILE, TILE), F32), unroll=slabs == group)
        mass = member_ref[i, 3:4, :]
        size = member_ref[i, 4:5, :]
        phi = mass * (2.0 / size) - jnp.sum(total.T, axis=0, keepdims=True)
        phi_ref[i] = phi
        return energy + mass * phi

    energy = lax.fori_loop(0, slabs, step, jnp.zeros((1, TILE), F32), unroll=8 if slabs == group else 1)
    energy_ref[...] = 0.5 * jnp.sum(energy, axis=1, keepdims=True)


def potential_rows(table_ref, count_ref, owner_ref, rest_ref):
    groups = count_ref.shape[1]
    used = rest_ref.shape[0] - 8
    rows = pl.ds(0, used)
    rest_ref[rows, :] = jnp.zeros((used, TILE), F32)
    lane = lax.broadcasted_iota(jnp.int32, (used, TILE), 1)
    place = lane + TILE * lax.broadcasted_iota(jnp.int32, (used, TILE), 0)

    def step(k, start):
        count = count_ref[0, k]
        value = pltpu.roll(table_ref[owner_ref[0, k]], start % TILE, 1)
        inside = (place >= start) & (place < start + count)
        rest_ref[rows, :] = jnp.where(inside, value, rest_ref[rows, :])
        return start + count

    lax.fori_loop(0, groups, step, jnp.int32(0), unroll=math.gcd(groups, 8))


def final_kernel(dens_ref, rest_ref, out_ref, pot_ref, energy_ref):
    used = rest_ref.shape[0] - 8
    out_ref[...] = dens_ref[...]
    pot_ref[pl.ds(0, used), :] = rest_ref[pl.ds(0, used), :]
    if used < pot_ref.shape[0]:
        pot_ref[pl.ds(used, pot_ref.shape[0] - used), :] = jnp.zeros((pot_ref.shape[0] - used, TILE), F32)
    energy_ref[...] = rest_ref[pl.ds(used, 1), pl.ds(0, 1)]


def per_device(positions, masses, smoothing, block_lists, block_counts, group_owner):
    row_count = masses.shape[1]
    blocks = row_count // TILE
    slabs = lax.axis_size("slab")
    grps = lax.axis_size("grp")
    particles = (
        positions[0].reshape(3, blocks, TILE),
        masses.reshape(blocks, TILE),
        smoothing.reshape(blocks, TILE),
    )
    grid_shape = jax.ShapeDtypeStruct((blocks, TILE), F32)
    dma = pltpu.SemaphoreType.DMA
    used = min(block_counts.shape[1], blocks)
    density, rest = pl.pallas_call(
        functools.partial(main_kernel, slabs, grps),
        out_shape=(grid_shape, jax.ShapeDtypeStruct((used + 8, TILE), F32)),
        in_specs=[ANY, ANY, ANY, SMEM, SMEM, SMEM],
        out_specs=(VMEM, VMEM),
        scratch_shapes=[
            pltpu.VMEM((slabs, 1, TILE), F32),
            pltpu.VMEM((blocks, TILE), F32),
            pltpu.VMEM((1, 1), F32),
            pltpu.VMEM((3, blocks, TILE), F32),
            pltpu.VMEM((blocks, TILE), F32),
            pltpu.VMEM((blocks, TILE), F32),
            pltpu.VMEM((3, blocks, TILE), F32),
            pltpu.VMEM((blocks, TILE), F32),
            pltpu.VMEM((blocks, TILE), F32),
            pltpu.VMEM((slabs, 8, TILE), F32),
            pltpu.VMEM((slabs, 8, TILE), F32),
            pltpu.VMEM((slabs, 1, TILE), F32),
            pltpu.VMEM((KX * blocks, TILE), F32),
            pltpu.VMEM((blocks, TILE), F32),
            pltpu.VMEM((blocks, TILE, DEPTH), HALF),
            pltpu.VMEM((blocks, DEPTH, 3 * TILE), HALF),
            pltpu.VMEM((blocks, TILE, DEPTH), HALF),
            pltpu.VMEM((KO * TILE, 3 * TILE), F32),
            pltpu.VMEM((KO * TILE, 3 * TILE), F32),
            pltpu.VMEM((KX * TILE, 3 * TILE), F32),
            pltpu.VMEM((KX * TILE, 3 * TILE), F32),
            pltpu.VMEM((slabs, TILE, 48), HALF),
            pltpu.VMEM((48, slabs * TILE), HALF),
            pltpu.VMEM((PLANES, blocks, TILE), F32),
            dma((3,)),
            dma((slabs,)),
            dma((slabs,)),
            dma((slabs,)),
            dma((slabs,)),
            dma((3,)),
            dma((3,)),
            dma,
            dma,
        ],
        compiler_params=pltpu.CompilerParams(
            collective_id=0,
            has_side_effects=True,
        ),
    )(*particles, block_lists[0].T, block_counts, group_owner)
    density, potential, energy = pl.pallas_call(
        final_kernel,
        out_shape=(grid_shape, grid_shape, jax.ShapeDtypeStruct((1, 1), F32)),
        in_specs=[VMEM, VMEM],
        out_specs=(VMEM, VMEM, VMEM),
    )(density, rest)
    return (density.reshape(1, row_count), potential.reshape(1, row_count), energy)


def solution(mesh):
    placed = (
        P(("slab", "grp"), None, None),
        P(("slab", "grp"), None),
        P(("slab", "grp"), None),
        P(("slab", "grp"), None, None),
        P(("slab", "grp"), None),
        P("grp", None),
    )
    return jax.shard_map(
        per_device,
        mesh=mesh,
        in_specs=placed,
        out_specs=(P(("slab", "grp"), None), P(("slab", "grp"), None), P("grp", "slab")),
        check_vma=False,
    )
```
